128 devices in a mesh: grp: 8 (over z, core), sub: 16 (over x, y).
Axes of the slice: x: 4, y: 4, z: 4, core: 2. Of those that a mesh axis runs over, the one named last changes fastest.
Arguments:
- rhs: float32 [96, 131072], P(None, ('grp', 'sub')), may hold values from -13 to 13
- blocks: bfloat16 [16384, 6656], P(('grp', 'sub')), may hold values from -0.05 to 0.45, as said below
- owners: int32 [16384, 1], P(('grp', 'sub')), may hold values from 0 to 7; in each aligned block of 128 rows (0 to 127, 128 to 255, ...) at most 48 rows name the same one
- conn: int32 [16384, 27], P(('grp', 'sub')), may hold values from 0 to 16383, as said below
Outputs:
- solution: float32 [96, 131072], P(None, ('grp', 'sub'))
- residual: float32 [96, 131072], P(None, ('grp', 'sub'))
The draws below stay inside these ranges and needn't reach their ends.
Inputs may be any that keep to these rules, and one draw needn't show every extreme that they name: `blocks`: entries at positions 6561 and beyond are zero. `owners`: in each device's 128 rows at most 48 name the same column. `conn`: A column's nodes form layers of 128 nodes, node n in layer n // 128. An element in the rows of the device at position s along sub touches three consecutive layers, all within nodes s * 1024 to (s + 1) * 1024 + 2 * 128 - 1 of its column (within the column).
All inputs are finite; a program needn't handle non-finite values.
Results may differ from the reference program's by a relative error of at most 0.0075.
Values may be sent and summed in bfloat16 or wider, within the bound.
A program may use at most 192 MiB of HBM per device.

```python
import math
import jax
import jax.numpy as jnp
import numpy as np
from jax import lax

NRHS = 32
KK = 6656
STEPS = 2
HELD = 128
CAP = 48
NODES_G = 16384
NODES = 131072
BLOCKS = 16384
N_GRP = 8
N_SUB = 16


def draw_rhs(key, part):
    position = jnp.arange(NODES, dtype=jnp.float32) / NODES
    layers = NODES // HELD
    layer_key, node_key = jax.random.split(key)
    common = 0.8 * jnp.clip(jax.random.normal(layer_key, (3 * NRHS, layers), jnp.float32), -2.5, 2.5)
    rough = 0.6 * jnp.clip(jax.random.normal(node_key, (3 * NRHS, NODES), jnp.float32), -4.0, 4.0)
    base = jnp.clip(jnp.repeat(common, HELD, axis=1) + rough, -4.0, 4.0)
    factor = 1.0 + 2.0 * position
    return base * factor[None, :]


def draw_blocks(key, part):
    total = N_GRP * N_SUB * HELD
    first_key, second_key = jax.random.split(key)
    cell = jnp.arange(KK, dtype=jnp.int32)
    row_index = cell // 81
    col_index = cell % 81
    inside = cell < 6561
    offdiag = jnp.clip(0.006 + 0.006 * jax.random.normal(first_key, (total, KK), jnp.float32), -0.05, 0.05)
    diagonal = jax.random.uniform(second_key, (total, KK), jnp.float32, 0.2, 0.4)
    values = jnp.where((row_index == col_index)[None, :], diagonal, offdiag)
    return jnp.where(inside[None, :], values, 0.0).astype(jnp.bfloat16)


def draw_conn(key, part):
    total = N_GRP * N_SUB * HELD
    width = HELD // 4
    layer_key, across_key, depth_key = jax.random.split(jax.random.fold_in(key, 7), 3)
    row = jnp.arange(total, dtype=jnp.int32)
    share = row // HELD % N_SUB
    top = jnp.where(share == N_SUB - 1, 6, 8).astype(jnp.int32)
    layer = jax.random.randint(layer_key, (total,), 0, top, dtype=jnp.int32)
    within = row % HELD
    layer = jnp.where(within == 0, 0, jnp.where(within == 1, top - 1, layer)).astype(jnp.int32)
    across = jax.random.randint(across_key, (total,), 0, 4, dtype=jnp.int32)
    depth = jax.random.randint(depth_key, (total,), 0, width, dtype=jnp.int32)
    corner = jnp.arange(27, dtype=jnp.int32)
    step_layer = corner // 9
    step_across = corner // 3 % 3
    step_depth = corner % 3
    node_layer = share[:, None] * 8 + layer[:, None] + step_layer[None, :]
    node_across = (across[:, None] + step_across[None, :]) % 4
    node_depth = (depth[:, None] + step_depth[None, :]) % width
    return (node_layer * HELD + node_across * width + node_depth).astype(jnp.int32)


def shared_out(rng, own, number, rows, number_of, top, most, lean):
    order = jax.random.permutation(rng, number_of)
    heavy_load, usual = portions_of(number_of, rows * top, most, lean, True), portions_of(number_of, rows * top, most, lean, False)
    places = jnp.arange(number_of)

    def named(tallies, rotation):
        used = int((tallies > 0).sum())
        fixed = max(1, used // 4)
        moved = fixed + (places - fixed + rotation * (used - fixed)) % max(1, number_of - fixed)
        return jnp.zeros((number_of,), jnp.int32).at[order[jnp.where(places < fixed, places, moved)]].set(jnp.asarray(tallies, jnp.int32))

    tallies = jnp.where(number % 4 == 0, named(heavy_load, number // 4), named(usual, number - number // 4 - 1))
    mixed = jax.random.permutation(jax.random.fold_in(own, 3), number_of)
    donor, taker = mixed[0:number_of // 2 * 2:2], mixed[1:number_of // 2 * 2:2]
    margin = jnp.minimum(tallies[donor] - 1, most - tallies[taker]) // 2
    margin = jnp.where((donor == order[0]) | (taker == order[0]) | (tallies[taker] == 0), 0, jnp.maximum(margin, 0))
    moved = jax.random.randint(jax.random.fold_in(own, 4), (number_of // 2,), 0, 1 << 20) % (margin + 1)
    tallies = tallies.at[donor].add(-moved).at[taker].add(moved)
    members = jnp.searchsorted(jnp.cumsum(tallies), jnp.arange(rows * top), side="right").astype(jnp.int32)
    listing = members.reshape(top, rows).T
    listing = listing[jax.random.permutation(jax.random.fold_in(own, 1), rows)]
    rotation = jax.random.randint(jax.random.fold_in(own, 2), (rows, 1), 0, top)
    return jnp.take_along_axis(listing, (jnp.arange(top)[None, :] + rotation) % top, axis=1)


def portions_of(number_of, total, most, skew, full):
    loads = [(1 << 20) // math.isqrt(rank ** skew) + 1 for rank in range(1, number_of + 1)]
    largest = most if full else min(most, max(-(-total // number_of), total * loads[0] // sum(loads)))
    least = 1 if total - largest >= number_of - 1 else 0
    holding, spare = [largest] + [least] * (number_of - 1), total - largest - least * (number_of - 1)
    while spare > 0:
        movable = [i for i in range(1, number_of) if holding[i] < largest] or [i for i in range(1, number_of) if holding[i] < most]
        mass, budget = sum([loads[i] for i in movable]), spare
        for i in movable:
            extra = min(most - holding[i], max(1, budget * loads[i] // mass), spare)
            holding[i] = holding[i] + extra
            spare = spare - extra
    return np.array(holding)


def setup_inputs(seed: int = 0) -> dict:
    arg_keys = jax.random.split(jax.random.key(seed), 5)
    rhs = draw_rhs(jax.random.fold_in(arg_keys[4], 71), 0)
    blocks = draw_blocks(jax.random.fold_in(arg_keys[4], 71), 0)
    owners_keys = jax.random.split(jax.random.fold_in(arg_keys[2], 1), BLOCKS // HELD)
    owners_turns = jax.random.permutation(jax.random.fold_in(arg_keys[2], 3), BLOCKS // HELD)
    owners = jax.vmap(lambda own, number: shared_out(jax.random.fold_in(arg_keys[2], 2), own, number, HELD, N_GRP, 1, CAP, 2))(owners_keys, owners_turns).reshape((BLOCKS, 1))
    conn = draw_conn(jax.random.fold_in(arg_keys[4], 71), 0)
    return dict(rhs=rhs, blocks=blocks, owners=owners, conn=conn)


def assemble(rounded, blocks, nodes_index):
    total = blocks.shape[0]
    batch = HELD * min(N_GRP * N_SUB, 8)
    count = total // batch
    rows = rounded.shape[0]

    def one_batch(acc, number):
        part = lax.dynamic_slice_in_dim(blocks, number * batch, batch, 0).astype(jnp.float32)
        node_links = lax.dynamic_slice_in_dim(nodes_index, number * batch, batch, 0).reshape(-1)
        matrix = part[:, :6561].reshape(batch, 27, 3, 27, 3)
        picked = jnp.take(rounded, node_links, axis=1).astype(jnp.float32).reshape(3, rows // 3, batch, 27)
        result = jnp.einsum("spcqd,cosp->dosq", matrix, picked, precision=lax.Precision.HIGHEST)
        return acc.at[:, node_links].add(result.reshape(rows, -1)), None

    start = jnp.zeros(rounded.shape, jnp.float32)
    acc, unused = lax.scan(one_batch, start, jnp.arange(count, dtype=jnp.int32))
    return acc


def column_sums(first, second):
    return jnp.sum((first * second).reshape(3, -1, first.shape[1]), axis=(0, 2))


def reference(rhs, blocks, owners, conn):
    nodes_index = (owners[:, 0:1] * NODES_G + conn).astype(jnp.int32)
    solution = jnp.zeros(rhs.shape, jnp.float32)
    residual = rhs
    for step in range(STEPS):
        rounded = residual.astype(jnp.bfloat16)
        image = assemble(rounded, blocks, nodes_index)
        along = column_sums(residual, image)
        energy = column_sums(image, image)
        alpha = along / (energy + 1e-6)
        scale_rows = jnp.tile(alpha, 3)[:, None]
        solution = solution + scale_rows * residual
        residual = residual - scale_rows * image
    return solution, residual
```

```python
import jax
import jax.numpy as jnp
from jax import lax
from jax.sharding import PartitionSpec as P

STEPS = 2


epsilon = 1e-06


def passed_along(block, axis, distance):
    devices = range(lax.axis_size(axis))
    route = [(i - distance, i) for i in devices if i - distance in devices]
    return lax.ppermute(block, axis, route)


def place_blocks(blocks, owners, conn, groups, capacity):
    owner_group = owners[:, 0]
    onehot = (owner_group[:, None] == jnp.arange(groups, dtype=jnp.int32)[None, :]).astype(
        jnp.int32
    )
    before = jnp.cumsum(onehot, axis=0) - onehot
    position = jnp.sum(before * onehot, axis=1)
    target = owner_group * capacity + position
    send_blocks = (
        jnp.zeros((groups * capacity, blocks.shape[1]), blocks.dtype).at[target].set(blocks)
    )
    send_links = jnp.zeros((groups * capacity, conn.shape[1]), jnp.int32).at[target].set(conn)
    return (send_blocks.reshape(groups, capacity, -1), send_links.reshape(groups, capacity, -1))


def window_product(matrix_groups, link_groups, field):
    rows = field.shape[0]
    window = field.shape[1]
    places = jnp.arange(window, dtype=jnp.int32)

    def one_group(acc, pair):
        matrix, links = pair
        slot_count = matrix.shape[0]
        selector = (links[:, None] == places[None, :]).astype(jnp.bfloat16)
        picked = jnp.einsum(
            "rw,lw->rl", field, selector, preferred_element_type=jnp.float32
        ).astype(jnp.bfloat16)
        picked = picked.reshape(3, rows // 3, slot_count, 27)
        result = jnp.einsum("spcqd,cosp->dosq", matrix, picked, preferred_element_type=jnp.float32)
        result = result.reshape(rows, slot_count * 27)
        high_part = result.astype(jnp.bfloat16)
        low_part = (result - high_part.astype(jnp.float32)).astype(jnp.bfloat16)
        acc = acc + jnp.dot(high_part, selector, preferred_element_type=jnp.float32)
        acc = acc + jnp.dot(low_part, selector, preferred_element_type=jnp.float32)
        return (acc, None)

    start = jnp.zeros((rows, window), jnp.float32)
    acc, unused = lax.scan(one_group, start, (matrix_groups, link_groups))
    return acc


def total_over_devices(value):
    axes = ("grp", "sub")
    count = lax.axis_size(axes)
    for bit in range(count.bit_length() - 1):
        pairs = [(i, i ^ (1 << bit)) for i in range(count)]
        value = value + lax.ppermute(value, axes, pairs)
    return value


def column_sums(first, second):
    return jnp.sum((first * second).reshape(3, -1, first.shape[1]), axis=(0, 2))


def update(solution, residual, image, along, energy):
    alpha = along / (energy + epsilon)
    scale_rows = jnp.tile(alpha, 3)[:, None]
    return (solution + scale_rows * residual, residual - scale_rows * image)


def shards(rhs, blocks, owners, conn):
    groups = lax.axis_size("grp")
    held = blocks.shape[0]
    capacity = max(2, 3 * held // 8)
    send_blocks, send_links = place_blocks(blocks, owners, conn, groups, capacity)
    got_blocks, got_links = (
        lax.all_to_all(send_blocks, "grp", split_axis=0, concat_axis=0, tiled=True),
        lax.all_to_all(send_links, "grp", split_axis=0, concat_axis=0, tiled=True),
    )
    matrix_groups = got_blocks[:, :, :6561].reshape(groups, capacity, 27, 3, 27, 3)
    residual = rhs
    solution = jnp.zeros(rhs.shape, jnp.float32)
    own_count = rhs.shape[1]
    band_width = 2 * held
    local_links = jnp.clip(
        got_links - lax.axis_index("sub") * own_count, 0, own_count + band_width - 1
    ).astype(jnp.int32)
    link_groups = local_links.reshape(groups, capacity * 27)
    for step in range(STEPS):
        rounded = residual.astype(jnp.bfloat16)
        upper = passed_along(rounded[:, :band_width], "sub", -1)
        field = jnp.concatenate([rounded, upper], axis=1)
        partial_sum = window_product(matrix_groups, link_groups, field)
        incoming = passed_along(partial_sum[:, own_count:], "sub", 1)
        image = partial_sum[:, :own_count] + jnp.pad(
            incoming, ((0, 0), (0, own_count - band_width))
        )
        sums = total_over_devices(
            jnp.stack([column_sums(residual, image), column_sums(image, image)])
        )
        along, energy = sums[0], sums[1]
        solution, residual = update(solution, residual, image, along, energy)
    return (solution, residual)


def solution(mesh):
    return jax.shard_map(
        shards,
        mesh=mesh,
        in_specs=(
            P(None, ("grp", "sub")),
            P(("grp", "sub"), None),
            P(("grp", "sub"), None),
            P(("grp", "sub"), None),
        ),
        out_specs=(P(None, ("grp", "sub")), P(None, ("grp", "sub"))),
        check_vma=False,
    )
```

```python
import jax
import jax.numpy as jnp
from jax import lax
from jax.sharding import PartitionSpec as P

STEPS = 2


epsilon = 1e-06


def passed_along(block, axis, distance):
    devices = range(lax.axis_size(axis))
    route = [(i - distance, i) for i in devices if i - distance in devices]
    return lax.ppermute(block, axis, route)


def place_blocks(blocks, owners, conn, groups, capacity):
    owner_group = owners[:, 0]
    onehot = (owner_group[:, None] == jnp.arange(groups, dtype=jnp.int32)[None, :]).astype(
        jnp.int32
    )
    before = jnp.cumsum(onehot, axis=0) - onehot
    position = jnp.sum(before * onehot, axis=1)
    target = owner_group * capacity + position
    send_blocks = (
        jnp.zeros((groups * capacity, blocks.shape[1]), blocks.dtype).at[target].set(blocks)
    )
    send_links = jnp.zeros((groups * capacity, conn.shape[1]), jnp.int32).at[target].set(conn)
    return (send_blocks.reshape(groups, capacity, -1), send_links.reshape(groups, capacity, -1))


def element_products(matrices, selector, field):
    rows = field.shape[0]
    count = matrices.shape[0]
    picked = lax.dot_general(
        selector, field, (((0,), (1,)), ((), ())), preferred_element_type=jnp.float32
    ).astype(jnp.bfloat16)
    picked = picked.reshape(count, 81, rows // 3)
    result = jnp.einsum("sab,sao->sbo", matrices, picked, preferred_element_type=jnp.float32)
    result = result.reshape(count * 27, rows)
    high_part = result.astype(jnp.bfloat16)
    low_part = (result - high_part.astype(jnp.float32)).astype(jnp.bfloat16)
    acc = jnp.dot(selector, high_part, preferred_element_type=jnp.float32)
    acc = acc + jnp.dot(selector, low_part, preferred_element_type=jnp.float32)
    return acc.T


def total_over_devices(value):
    axes = ("grp", "sub")
    count = lax.axis_size(axes)
    for bit in range(count.bit_length() - 1):
        pairs = [(i, i ^ (1 << bit)) for i in range(count)]
        value = value + lax.ppermute(value, axes, pairs)
    return value


def column_sums(first, second):
    return jnp.sum((first * second).reshape(3, -1, first.shape[1]), axis=(0, 2))


def update(solution, residual, image, along, energy):
    alpha = along / (energy + epsilon)
    scale_rows = jnp.tile(alpha, 3)[:, None]
    return (solution + scale_rows * residual, residual - scale_rows * image)


def shards(rhs, blocks, owners, conn):
    groups = lax.axis_size("grp")
    held = blocks.shape[0]
    capacity = max(2, 3 * held // 8)
    send_blocks, send_links = place_blocks(blocks, owners, conn, groups, capacity)
    got_blocks, got_links = (
        lax.all_to_all(send_blocks, "grp", split_axis=0, concat_axis=0, tiled=True),
        lax.all_to_all(send_links, "grp", split_axis=0, concat_axis=0, tiled=True),
    )
    matrices = got_blocks[:, :, :6561].reshape(groups * capacity, 81, 81)
    residual = rhs
    solution = jnp.zeros(rhs.shape, jnp.float32)
    own_count = rhs.shape[1]
    band_width = 2 * held
    local_links = jnp.clip(
        got_links - lax.axis_index("sub") * own_count, 0, own_count + band_width - 1
    ).astype(jnp.int32)
    places = jnp.arange(own_count + band_width, dtype=jnp.int32)
    selector = (places[:, None] == local_links.reshape(1, -1)).astype(jnp.bfloat16)
    for step in range(STEPS):
        rounded = residual.astype(jnp.bfloat16)
        upper = passed_along(rounded[:, :band_width], "sub", -1)
        field = jnp.concatenate([rounded, upper], axis=1)
        partial_sum = element_products(matrices, selector, field)
        incoming = passed_along(partial_sum[:, own_count:], "sub", 1)
        image = partial_sum[:, :own_count] + jnp.pad(
            incoming, ((0, 0), (0, own_count - band_width))
        )
        sums = total_over_devices(
            jnp.stack([column_sums(residual, image), column_sums(image, image)])
        )
        along, energy = sums[0], sums[1]
        solution, residual = update(solution, residual, image, along, energy)
    return (solution, residual)


def solution(mesh):
    return jax.shard_map(
        shards,
        mesh=mesh,
        in_specs=(
            P(None, ("grp", "sub")),
            P(("grp", "sub"), None),
            P(("grp", "sub"), None),
            P(("grp", "sub"), None),
        ),
        out_specs=(P(None, ("grp", "sub")), P(None, ("grp", "sub"))),
        check_vma=False,
    )
```

```python
import jax
import jax.numpy as jnp
from jax import lax
from jax.sharding import PartitionSpec as P

STEPS = 2


epsilon = 1e-06


def passed_along(block, axis, distance):
    devices = range(lax.axis_size(axis))
    route = [(i - distance, i) for i in devices if i - distance in devices]
    return lax.ppermute(block, axis, route)


def place_blocks(blocks, owners, conn, groups, capacity):
    owner_group = owners[:, 0]
    onehot = (owner_group[:, None] == jnp.arange(groups, dtype=jnp.int32)[None, :]).astype(
        jnp.int32
    )
    before = jnp.cumsum(onehot, axis=0) - onehot
    position = jnp.sum(before * onehot, axis=1)
    target = owner_group * capacity + position
    send_blocks = (
        jnp.zeros((groups * capacity, blocks.shape[1]), blocks.dtype).at[target].set(blocks)
    )
    send_links = jnp.zeros((groups * capacity, conn.shape[1]), jnp.int32).at[target].set(conn)
    return (send_blocks.reshape(groups, capacity, -1), send_links.reshape(groups, capacity, -1))


def element_products(matrices, selector, field):
    rows = field.shape[0]
    count = matrices.shape[0]
    picked = lax.dot_general(
        selector, field, (((0,), (1,)), ((), ())), preferred_element_type=jnp.float32
    ).astype(jnp.bfloat16)
    picked = picked.reshape(count, 81, rows // 3)
    result = jnp.einsum("sab,sao->sbo", matrices, picked, preferred_element_type=jnp.float32)
    result = result.reshape(count * 27, rows)
    high_part = result.astype(jnp.bfloat16)
    low_part = (result - high_part.astype(jnp.float32)).astype(jnp.bfloat16)
    parts = jnp.concatenate([high_part, low_part], axis=1)
    acc = jnp.dot(selector, parts, preferred_element_type=jnp.float32)
    return (acc[:, :rows] + acc[:, rows:]).T


def total_over_devices(value):
    axes = ("grp", "sub")
    count = lax.axis_size(axes)
    for bit in range(count.bit_length() - 1):
        pairs = [(i, i ^ (1 << bit)) for i in range(count)]
        value = value + lax.ppermute(value, axes, pairs)
    return value


def column_sums(first, second):
    return jnp.sum((first * second).reshape(3, -1, first.shape[1]), axis=(0, 2))


def update(solution, residual, image, along, energy):
    alpha = along / (energy + epsilon)
    scale_rows = jnp.tile(alpha, 3)[:, None]
    return (solution + scale_rows * residual, residual - scale_rows * image)


def shards(rhs, blocks, owners, conn):
    groups = lax.axis_size("grp")
    held = blocks.shape[0]
    capacity = max(2, 3 * held // 8)
    send_blocks, send_links = place_blocks(blocks, owners, conn, groups, capacity)
    got_blocks, got_links = (
        lax.all_to_all(send_blocks, "grp", split_axis=0, concat_axis=0, tiled=True),
        lax.all_to_all(send_links, "grp", split_axis=0, concat_axis=0, tiled=True),
    )
    matrices = got_blocks[:, :, :6561].reshape(groups * capacity, 81, 81)
    residual = rhs
    solution = jnp.zeros(rhs.shape, jnp.float32)
    own_count = rhs.shape[1]
    band_width = 2 * held
    local_links = jnp.clip(
        got_links - lax.axis_index("sub") * own_count, 0, own_count + band_width - 1
    ).astype(jnp.int32)
    places = jnp.arange(own_count + band_width, dtype=jnp.int32)
    selector = (places[:, None] == local_links.reshape(1, -1)).astype(jnp.bfloat16)
    for step in range(STEPS):
        rounded = residual.astype(jnp.bfloat16)
        upper = passed_along(rounded[:, :band_width], "sub", -1)
        field = jnp.concatenate([rounded, upper], axis=1)
        partial_sum = element_products(matrices, selector, field)
        incoming = passed_along(partial_sum[:, own_count:], "sub", 1)
        image = partial_sum[:, :own_count] + jnp.pad(
            incoming, ((0, 0), (0, own_count - band_width))
        )
        sums = total_over_devices(
            jnp.stack([column_sums(residual, image), column_sums(image, image)])
        )
        along, energy = sums[0], sums[1]
        solution, residual = update(solution, residual, image, along, energy)
    return (solution, residual)


def solution(mesh):
    return jax.shard_map(
        shards,
        mesh=mesh,
        in_specs=(
            P(None, ("grp", "sub")),
            P(("grp", "sub"), None),
            P(("grp", "sub"), None),
            P(("grp", "sub"), None),
        ),
        out_specs=(P(None, ("grp", "sub")), P(None, ("grp", "sub"))),
        check_vma=False,
    )
```

```python
import functools

import jax
import jax.numpy as jnp
from jax import lax
from jax.experimental import pallas as pl
from jax.experimental.pallas import tpu as pltpu
from jax.sharding import PartitionSpec as P

MESH = pl.DeviceIdType.MESH

STEPS = 2


epsilon = 1e-06


def passed_along(block, axis, distance):
    devices = range(lax.axis_size(axis))
    route = [(i - distance, i) for i in devices if i - distance in devices]
    return lax.ppermute(block, axis, route)


def place_blocks(blocks, owners, conn, groups, capacity):
    owner_group = owners[:, 0]
    onehot = (owner_group[:, None] == jnp.arange(groups, dtype=jnp.int32)[None, :]).astype(
        jnp.int32
    )
    before = jnp.cumsum(onehot, axis=0) - onehot
    position = jnp.sum(before * onehot, axis=1)
    target = owner_group * capacity + position
    send_blocks = (
        jnp.zeros((groups * capacity, blocks.shape[1]), blocks.dtype).at[target].set(blocks)
    )
    send_links = jnp.zeros((groups * capacity, conn.shape[1]), jnp.int32).at[target].set(conn)
    return (send_blocks.reshape(groups, capacity, -1), send_links.reshape(groups, capacity, -1))


def element_products(matrices, selector, field):
    rows = field.shape[0]
    count = matrices.shape[0]
    picked = lax.dot_general(
        selector, field, (((0,), (1,)), ((), ())), preferred_element_type=jnp.float32
    ).astype(jnp.bfloat16)
    picked = picked.reshape(count, 81, rows // 3)
    result = jnp.einsum("sab,sao->sbo", matrices, picked, preferred_element_type=jnp.float32)
    result = result.reshape(count * 27, rows)
    high_part = result.astype(jnp.bfloat16)
    low_part = (result - high_part.astype(jnp.float32)).astype(jnp.bfloat16)
    parts = jnp.concatenate([high_part, low_part], axis=1)
    acc = jnp.dot(selector, parts, preferred_element_type=jnp.float32)
    return (acc[:, :rows] + acc[:, rows:]).T


def partner_of(me, bit, n_sub):
    span = 1 << bit
    partner = me + span - 2 * span * ((me // span) % 2)
    return (partner // n_sub, partner % n_sub)


def butterfly_kernel(n_sub, rounds, x_ref, o_ref, sent, got, send_sem, recv_sem):
    me = lax.axis_index("grp") * n_sub + lax.axis_index("sub")
    barrier = pltpu.get_barrier_semaphore()
    for bit in range(rounds):
        pl.semaphore_signal(
            barrier, inc=1, device_id=partner_of(me, bit, n_sub), device_id_type=MESH
        )
    pl.semaphore_wait(barrier, rounds)
    acc = x_ref[...]
    for bit in range(rounds):
        sent[bit] = acc
        copy = pltpu.make_async_remote_copy(
            src_ref=sent.at[bit],
            dst_ref=got.at[bit],
            send_sem=send_sem.at[bit],
            recv_sem=recv_sem.at[bit],
            device_id=partner_of(me, bit, n_sub),
            device_id_type=MESH,
        )
        copy.start()
        copy.wait()
        acc = acc + got[bit]
    o_ref[...] = acc


def total_over_devices(value, call):
    n_sub = lax.axis_size("sub")
    rounds = (lax.axis_size("grp") * n_sub).bit_length() - 1
    flat = value.reshape(-1)
    block = jnp.zeros((8, 128), jnp.float32).reshape(-1).at[: flat.shape[0]].set(flat)
    block = block.reshape(8, 128)
    summed = pl.pallas_call(
        functools.partial(butterfly_kernel, n_sub, rounds),
        out_shape=jax.ShapeDtypeStruct((8, 128), jnp.float32),
        in_specs=[pl.BlockSpec(memory_space=pltpu.VMEM)],
        out_specs=pl.BlockSpec(memory_space=pltpu.VMEM),
        scratch_shapes=[
            pltpu.VMEM((rounds, 8, 128), jnp.float32),
            pltpu.VMEM((rounds, 8, 128), jnp.float32),
            pltpu.SemaphoreType.DMA((rounds,)),
            pltpu.SemaphoreType.DMA((rounds,)),
        ],
        compiler_params=pltpu.CompilerParams(collective_id=call, has_side_effects=True),
    )(block)
    return summed.reshape(-1)[: flat.shape[0]].reshape(value.shape)


def column_sums(first, second):
    return jnp.sum((first * second).reshape(3, -1, first.shape[1]), axis=(0, 2))


def update(solution, residual, image, along, energy):
    alpha = along / (energy + epsilon)
    scale_rows = jnp.tile(alpha, 3)[:, None]
    return (solution + scale_rows * residual, residual - scale_rows * image)


def shards(rhs, blocks, owners, conn):
    groups = lax.axis_size("grp")
    held = blocks.shape[0]
    capacity = max(2, 3 * held // 8)
    send_blocks, send_links = place_blocks(blocks, owners, conn, groups, capacity)
    got_blocks, got_links = (
        lax.all_to_all(send_blocks, "grp", split_axis=0, concat_axis=0, tiled=True),
        lax.all_to_all(send_links, "grp", split_axis=0, concat_axis=0, tiled=True),
    )
    matrices = got_blocks[:, :, :6561].reshape(groups * capacity, 81, 81)
    residual = rhs
    solution = jnp.zeros(rhs.shape, jnp.float32)
    own_count = rhs.shape[1]
    band_width = 2 * held
    local_links = jnp.clip(
        got_links - lax.axis_index("sub") * own_count, 0, own_count + band_width - 1
    ).astype(jnp.int32)
    places = jnp.arange(own_count + band_width, dtype=jnp.int32)
    selector = (places[:, None] == local_links.reshape(1, -1)).astype(jnp.bfloat16)
    for step in range(STEPS):
        rounded = residual.astype(jnp.bfloat16)
        upper = passed_along(rounded[:, :band_width], "sub", -1)
        field = jnp.concatenate([rounded, upper], axis=1)
        partial_sum = element_products(matrices, selector, field)
        incoming = passed_along(partial_sum[:, own_count:], "sub", 1)
        image = partial_sum[:, :own_count] + jnp.pad(
            incoming, ((0, 0), (0, own_count - band_width))
        )
        sums = total_over_devices(
            jnp.stack([column_sums(residual, image), column_sums(image, image)]), step
        )
        along, energy = sums[0], sums[1]
        solution, residual = update(solution, residual, image, along, energy)
    return (solution, residual)


def solution(mesh):
    return jax.shard_map(
        shards,
        mesh=mesh,
        in_specs=(
            P(None, ("grp", "sub")),
            P(("grp", "sub"), None),
            P(("grp", "sub"), None),
            P(("grp", "sub"), None),
        ),
        out_specs=(P(None, ("grp", "sub")), P(None, ("grp", "sub"))),
        check_vma=False,
    )
```

```python
import functools

import jax
import jax.numpy as jnp
from jax import lax
from jax.experimental import pallas as pl
from jax.experimental.pallas import tpu as pltpu
from jax.sharding import PartitionSpec as P

MESH = pl.DeviceIdType.MESH

STEPS = 2


epsilon = 1e-06


def passed_along(block, axis, distance):
    devices = range(lax.axis_size(axis))
    route = [(i - distance, i) for i in devices if i - distance in devices]
    return lax.ppermute(block, axis, route)


def place_blocks(blocks, owners, conn, groups, capacity):
    owner_group = owners[:, 0]
    onehot = (owner_group[:, None] == jnp.arange(groups, dtype=jnp.int32)[None, :]).astype(
        jnp.int32
    )
    before = jnp.cumsum(onehot, axis=0) - onehot
    position = jnp.sum(before * onehot, axis=1)
    target = owner_group * capacity + position
    send_blocks = (
        jnp.zeros((groups * capacity, blocks.shape[1]), blocks.dtype).at[target].set(blocks)
    )
    send_links = jnp.zeros((groups * capacity, conn.shape[1]), jnp.int32).at[target].set(conn)
    return (send_blocks.reshape(groups, capacity, -1), send_links.reshape(groups, capacity, -1))


def element_products(matrices, selector, field):
    rows = field.shape[0]
    count = matrices.shape[0]
    picked = lax.dot_general(
        selector, field, (((0,), (1,)), ((), ())), preferred_element_type=jnp.float32
    ).astype(jnp.bfloat16)
    picked = picked.reshape(count, 81, rows // 3)
    result = jnp.einsum("sab,sao->sbo", matrices, picked, preferred_element_type=jnp.float32)
    result = result.reshape(count * 27, rows)
    high_part = result.astype(jnp.bfloat16)
    low_part = (result - high_part.astype(jnp.float32)).astype(jnp.bfloat16)
    parts = jnp.concatenate([high_part, low_part], axis=1)
    acc = jnp.dot(selector, parts, preferred_element_type=jnp.float32)
    return (acc[:, :rows] + acc[:, rows:]).T


def gather_sum_kernel(n_grp, n_sub, x_ref, o_ref, slots, send_sem, recv_sem):
    my_grp = lax.axis_index("grp")
    my_sub = lax.axis_index("sub")
    barrier = pltpu.get_barrier_semaphore()
    for d in range(1, n_sub):
        target = (my_grp, (my_sub + d) % n_sub)
        pl.semaphore_signal(barrier, inc=1, device_id=target, device_id_type=MESH)
    for d in range(1, n_grp):
        target = ((my_grp + d) % n_grp, my_sub)
        pl.semaphore_signal(barrier, inc=1, device_id=target, device_id_type=MESH)
    pl.semaphore_wait(barrier, n_sub - 1 + n_grp - 1)

    def exchange(value, first, count, my_index, device_of):
        slots[first + my_index] = value
        sends = []
        for d in range(1, count):
            copy = pltpu.make_async_remote_copy(
                src_ref=slots.at[first + my_index],
                dst_ref=slots.at[first + my_index],
                send_sem=send_sem.at[first + d],
                recv_sem=recv_sem.at[first + my_index],
                device_id=device_of((my_index + d) % count),
                device_id_type=MESH,
            )
            copy.start()
            sends.append(copy)
        for d in range(1, count):
            source = (my_index + count - d) % count
            pltpu.make_async_remote_copy(
                src_ref=slots.at[first + source],
                dst_ref=slots.at[first + source],
                send_sem=send_sem.at[first + d],
                recv_sem=recv_sem.at[first + source],
                device_id=device_of(source),
                device_id_type=MESH,
            ).wait_recv()
        for copy in sends:
            copy.wait_send()
        total = slots[first]
        for i in range(1, count):
            total = total + slots[first + i]
        return total

    partial_sum = exchange(x_ref[...], 0, n_sub, my_sub, lambda i: (my_grp, i))
    o_ref[...] = exchange(partial_sum, n_sub, n_grp, my_grp, lambda i: (i, my_sub))


def total_over_devices(value, call):
    n_grp = lax.axis_size("grp")
    n_sub = lax.axis_size("sub")
    flat = value.reshape(-1)
    block = jnp.zeros((8 * 128,), jnp.float32).at[: flat.shape[0]].set(flat)
    block = block.reshape(8, 128)
    summed = pl.pallas_call(
        functools.partial(gather_sum_kernel, n_grp, n_sub),
        out_shape=jax.ShapeDtypeStruct((8, 128), jnp.float32),
        in_specs=[pl.BlockSpec(memory_space=pltpu.VMEM)],
        out_specs=pl.BlockSpec(memory_space=pltpu.VMEM),
        scratch_shapes=[
            pltpu.VMEM((n_sub + n_grp, 8, 128), jnp.float32),
            pltpu.SemaphoreType.DMA((n_sub + n_grp,)),
            pltpu.SemaphoreType.DMA((n_sub + n_grp,)),
        ],
        compiler_params=pltpu.CompilerParams(collective_id=call, has_side_effects=True),
    )(block)
    return summed.reshape(-1)[: flat.shape[0]].reshape(value.shape)


def column_sums(first, second):
    return jnp.sum((first * second).reshape(3, -1, first.shape[1]), axis=(0, 2))


def update(solution, residual, image, along, energy):
    alpha = along / (energy + epsilon)
    scale_rows = jnp.tile(alpha, 3)[:, None]
    return (solution + scale_rows * residual, residual - scale_rows * image)


def shards(rhs, blocks, owners, conn):
    groups = lax.axis_size("grp")
    held = blocks.shape[0]
    capacity = max(2, 3 * held // 8)
    send_blocks, send_links = place_blocks(blocks, owners, conn, groups, capacity)
    got_blocks, got_links = (
        lax.all_to_all(send_blocks, "grp", split_axis=0, concat_axis=0, tiled=True),
        lax.all_to_all(send_links, "grp", split_axis=0, concat_axis=0, tiled=True),
    )
    matrices = got_blocks[:, :, :6561].reshape(groups * capacity, 81, 81)
    residual = rhs
    solution = jnp.zeros(rhs.shape, jnp.float32)
    own_count = rhs.shape[1]
    band_width = 2 * held
    local_links = jnp.clip(
        got_links - lax.axis_index("sub") * own_count, 0, own_count + band_width - 1
    ).astype(jnp.int32)
    places = jnp.arange(own_count + band_width, dtype=jnp.int32)
    selector = (places[:, None] == local_links.reshape(1, -1)).astype(jnp.bfloat16)
    for step in range(STEPS):
        rounded = residual.astype(jnp.bfloat16)
        upper = passed_along(rounded[:, :band_width], "sub", -1)
        field = jnp.concatenate([rounded, upper], axis=1)
        partial_sum = element_products(matrices, selector, field)
        incoming = passed_along(partial_sum[:, own_count:], "sub", 1)
        image = partial_sum[:, :own_count] + jnp.pad(
            incoming, ((0, 0), (0, own_count - band_width))
        )
        sums = total_over_devices(
            jnp.stack([column_sums(residual, image), column_sums(image, image)]), step
        )
        along, energy = sums[0], sums[1]
        solution, residual = update(solution, residual, image, along, energy)
    return (solution, residual)


def solution(mesh):
    return jax.shard_map(
        shards,
        mesh=mesh,
        in_specs=(
            P(None, ("grp", "sub")),
            P(("grp", "sub"), None),
            P(("grp", "sub"), None),
            P(("grp", "sub"), None),
        ),
        out_specs=(P(None, ("grp", "sub")), P(None, ("grp", "sub"))),
        check_vma=False,
    )
```

```python
import functools

import jax
import jax.numpy as jnp
from jax import lax
from jax.experimental import pallas as pl
from jax.experimental.pallas import tpu as pltpu
from jax.sharding import PartitionSpec as P

MESH = pl.DeviceIdType.MESH

STEPS = 2


epsilon = 1e-06


def passed_along(block, axis, distance):
    devices = range(lax.axis_size(axis))
    route = [(i - distance, i) for i in devices if i - distance in devices]
    return lax.ppermute(block, axis, route)


def place_blocks(blocks, owners, conn, groups, capacity):
    owner_group = owners[:, 0]
    onehot = (owner_group[:, None] == jnp.arange(groups, dtype=jnp.int32)[None, :]).astype(
        jnp.int32
    )
    before = jnp.cumsum(onehot, axis=0) - onehot
    position = jnp.sum(before * onehot, axis=1)
    target = owner_group * capacity + position
    slots = jnp.arange(groups * capacity, dtype=jnp.int32)
    placement = (slots[:, None] == target[None, :]).astype(blocks.dtype)
    send_blocks = jnp.dot(placement, blocks, preferred_element_type=jnp.float32).astype(
        blocks.dtype
    )
    send_links = jnp.zeros((groups * capacity, conn.shape[1]), jnp.int32).at[target].set(conn)
    return (send_blocks.reshape(groups, capacity, -1), send_links.reshape(groups, capacity, -1))


def element_products(matrices, selector, field):
    rows = field.shape[0]
    count = matrices.shape[0]
    picked = lax.dot_general(
        selector, field, (((0,), (1,)), ((), ())), preferred_element_type=jnp.float32
    ).astype(jnp.bfloat16)
    picked = picked.reshape(count, 81, rows // 3)
    result = jnp.einsum("sab,sao->sbo", matrices, picked, preferred_element_type=jnp.float32)
    result = result.reshape(count * 27, rows)
    high_part = result.astype(jnp.bfloat16)
    low_part = (result - high_part.astype(jnp.float32)).astype(jnp.bfloat16)
    parts = jnp.concatenate([high_part, low_part], axis=1)
    acc = jnp.dot(selector, parts, preferred_element_type=jnp.float32)
    return (acc[:, :rows] + acc[:, rows:]).T


def gather_sum_kernel(n_grp, n_sub, x_ref, o_ref, slots, send_sem, recv_sem):
    my_grp = lax.axis_index("grp")
    my_sub = lax.axis_index("sub")
    barrier = pltpu.get_barrier_semaphore()
    for d in range(1, n_sub):
        target = (my_grp, (my_sub + d) % n_sub)
        pl.semaphore_signal(barrier, inc=1, device_id=target, device_id_type=MESH)
    for d in range(1, n_grp):
        target = ((my_grp + d) % n_grp, my_sub)
        pl.semaphore_signal(barrier, inc=1, device_id=target, device_id_type=MESH)
    pl.semaphore_wait(barrier, n_sub - 1 + n_grp - 1)

    def exchange(value, first, count, my_index, device_of):
        slots[first + my_index] = value
        sends = []
        for d in range(1, count):
            copy = pltpu.make_async_remote_copy(
                src_ref=slots.at[first + my_index],
                dst_ref=slots.at[first + my_index],
                send_sem=send_sem.at[first + d],
                recv_sem=recv_sem.at[first + my_index],
                device_id=device_of((my_index + d) % count),
                device_id_type=MESH,
            )
            copy.start()
            sends.append(copy)
        for d in range(1, count):
            source = (my_index + count - d) % count
            pltpu.make_async_remote_copy(
                src_ref=slots.at[first + source],
                dst_ref=slots.at[first + source],
                send_sem=send_sem.at[first + d],
                recv_sem=recv_sem.at[first + source],
                device_id=device_of(source),
                device_id_type=MESH,
            ).wait_recv()
        for copy in sends:
            copy.wait_send()
        total = slots[first]
        for i in range(1, count):
            total = total + slots[first + i]
        return total

    partial_sum = exchange(x_ref[...], 0, n_sub, my_sub, lambda i: (my_grp, i))
    o_ref[...] = exchange(partial_sum, n_sub, n_grp, my_grp, lambda i: (i, my_sub))


def total_over_devices(value, call):
    n_grp = lax.axis_size("grp")
    n_sub = lax.axis_size("sub")
    flat = value.reshape(-1)
    block = jnp.zeros((8 * 128,), jnp.float32).at[: flat.shape[0]].set(flat)
    block = block.reshape(8, 128)
    summed = pl.pallas_call(
        functools.partial(gather_sum_kernel, n_grp, n_sub),
        out_shape=jax.ShapeDtypeStruct((8, 128), jnp.float32),
        in_specs=[pl.BlockSpec(memory_space=pltpu.VMEM)],
        out_specs=pl.BlockSpec(memory_space=pltpu.VMEM),
        scratch_shapes=[
            pltpu.VMEM((n_sub + n_grp, 8, 128), jnp.float32),
            pltpu.SemaphoreType.DMA((n_sub + n_grp,)),
            pltpu.SemaphoreType.DMA((n_sub + n_grp,)),
        ],
        compiler_params=pltpu.CompilerParams(collective_id=call, has_side_effects=True),
    )(block)
    return summed.reshape(-1)[: flat.shape[0]].reshape(value.shape)


def column_sums(first, second):
    return jnp.sum((first * second).reshape(3, -1, first.shape[1]), axis=(0, 2))


def update(solution, residual, image, along, energy):
    alpha = along / (energy + epsilon)
    scale_rows = jnp.tile(alpha, 3)[:, None]
    return (solution + scale_rows * residual, residual - scale_rows * image)


def shards(rhs, blocks, owners, conn):
    groups = lax.axis_size("grp")
    held = blocks.shape[0]
    capacity = max(2, 3 * held // 8)
    send_blocks, send_links = place_blocks(blocks, owners, conn, groups, capacity)
    got_blocks, got_links = (
        lax.all_to_all(send_blocks, "grp", split_axis=0, concat_axis=0, tiled=True),
        lax.all_to_all(send_links, "grp", split_axis=0, concat_axis=0, tiled=True),
    )
    matrices = got_blocks[:, :, :6561].reshape(groups * capacity, 81, 81)
    residual = rhs
    solution = jnp.zeros(rhs.shape, jnp.float32)
    own_count = rhs.shape[1]
    band_width = 2 * held
    local_links = jnp.clip(
        got_links - lax.axis_index("sub") * own_count, 0, own_count + band_width - 1
    ).astype(jnp.int32)
    places = jnp.arange(own_count + band_width, dtype=jnp.int32)
    selector = (places[:, None] == local_links.reshape(1, -1)).astype(jnp.bfloat16)
    for step in range(STEPS):
        rounded = residual.astype(jnp.bfloat16)
        upper = passed_along(rounded[:, :band_width], "sub", -1)
        field = jnp.concatenate([rounded, upper], axis=1)
        partial_sum = element_products(matrices, selector, field)
        incoming = passed_along(partial_sum[:, own_count:], "sub", 1)
        image = partial_sum[:, :own_count] + jnp.pad(
            incoming, ((0, 0), (0, own_count - band_width))
        )
        sums = total_over_devices(
            jnp.stack([column_sums(residual, image), column_sums(image, image)]), step
        )
        along, energy = sums[0], sums[1]
        solution, residual = update(solution, residual, image, along, energy)
    return (solution, residual)


def solution(mesh):
    return jax.shard_map(
        shards,
        mesh=mesh,
        in_specs=(
            P(None, ("grp", "sub")),
            P(("grp", "sub"), None),
            P(("grp", "sub"), None),
            P(("grp", "sub"), None),
        ),
        out_specs=(P(None, ("grp", "sub")), P(None, ("grp", "sub"))),
        check_vma=False,
    )
```

```python
import functools

import jax
import jax.numpy as jnp
from jax import lax
from jax.experimental import pallas as pl
from jax.experimental.pallas import tpu as pltpu
from jax.sharding import PartitionSpec as P

MESH = pl.DeviceIdType.MESH

STEPS = 2


epsilon = 1e-06


def passed_along(block, axis, distance):
    devices = range(lax.axis_size(axis))
    route = [(i - distance, i) for i in devices if i - distance in devices]
    return lax.ppermute(block, axis, route)


def place_blocks(blocks, owners, conn, groups, capacity):
    owner_group = owners[:, 0]
    onehot = (owner_group[:, None] == jnp.arange(groups, dtype=jnp.int32)[None, :]).astype(
        jnp.int32
    )
    before = jnp.cumsum(onehot, axis=0) - onehot
    position = jnp.sum(before * onehot, axis=1)
    target = owner_group * capacity + position
    send_blocks = (
        jnp.zeros((groups * capacity, blocks.shape[1]), blocks.dtype).at[target].set(blocks)
    )
    send_links = jnp.zeros((groups * capacity, conn.shape[1]), jnp.int32).at[target].set(conn)
    return (send_blocks.reshape(groups, capacity, -1), send_links.reshape(groups, capacity, -1))


def element_products(matrices, selector, field):
    rows = field.shape[0]
    count = matrices.shape[0]
    picked = lax.dot_general(
        selector, field, (((0,), (1,)), ((), ())), preferred_element_type=jnp.float32
    ).astype(jnp.bfloat16)
    picked = picked.reshape(count, 81, rows // 3)
    result = jnp.einsum("sab,sao->sbo", matrices, picked, preferred_element_type=jnp.float32)
    result = result.reshape(count * 27, rows)
    high_part = result.astype(jnp.bfloat16)
    low_part = (result - high_part.astype(jnp.float32)).astype(jnp.bfloat16)
    parts = jnp.concatenate([high_part, low_part], axis=1)
    acc = jnp.dot(selector, parts, preferred_element_type=jnp.float32)
    return (acc[:, :rows] + acc[:, rows:]).T


def gather_sum_kernel(n_grp, n_sub, x_ref, o_ref, slots, send_sem, recv_sem):
    count = n_grp * n_sub
    me = lax.axis_index("grp") * n_sub + lax.axis_index("sub")

    def device_of(i):
        return (i // n_sub, i % n_sub)

    barrier = pltpu.get_barrier_semaphore()

    def greet(d, carry):
        pl.semaphore_signal(
            barrier, inc=1, device_id=device_of((me + d) % count), device_id_type=MESH
        )
        return carry

    lax.fori_loop(1, count, greet, 0)
    pl.semaphore_wait(barrier, count - 1)
    slots[me] = x_ref[...]

    def outgoing(d):
        return pltpu.make_async_remote_copy(
            src_ref=slots.at[me],
            dst_ref=slots.at[me],
            send_sem=send_sem.at[d],
            recv_sem=recv_sem.at[me],
            device_id=device_of((me + d) % count),
            device_id_type=MESH,
        )

    def send(d, carry):
        outgoing(d).start()
        return carry

    def receive(d, carry):
        source = (me + count - d) % count
        pltpu.make_async_remote_copy(
            src_ref=slots.at[source],
            dst_ref=slots.at[source],
            send_sem=send_sem.at[d],
            recv_sem=recv_sem.at[source],
            device_id=device_of(source),
            device_id_type=MESH,
        ).wait_recv()
        return carry

    def sent(d, carry):
        outgoing(d).wait_send()
        return carry

    lax.fori_loop(1, count, send, 0)
    lax.fori_loop(1, count, receive, 0)
    lax.fori_loop(1, count, sent, 0)
    o_ref[...] = lax.fori_loop(1, count, lambda i, acc: acc + slots[i], slots[0])


def total_over_devices(value, call):
    n_grp = lax.axis_size("grp")
    n_sub = lax.axis_size("sub")
    flat = value.reshape(-1)
    block = jnp.zeros((8 * 128,), jnp.float32).at[: flat.shape[0]].set(flat)
    block = block.reshape(8, 128)
    summed = pl.pallas_call(
        functools.partial(gather_sum_kernel, n_grp, n_sub),
        out_shape=jax.ShapeDtypeStruct((8, 128), jnp.float32),
        in_specs=[pl.BlockSpec(memory_space=pltpu.VMEM)],
        out_specs=pl.BlockSpec(memory_space=pltpu.VMEM),
        scratch_shapes=[
            pltpu.VMEM((n_grp * n_sub, 8, 128), jnp.float32),
            pltpu.SemaphoreType.DMA((n_grp * n_sub,)),
            pltpu.SemaphoreType.DMA((n_grp * n_sub,)),
        ],
        compiler_params=pltpu.CompilerParams(collective_id=call, has_side_effects=True),
    )(block)
    return summed.reshape(-1)[: flat.shape[0]].reshape(value.shape)


def column_sums(first, second):
    return jnp.sum((first * second).reshape(3, -1, first.shape[1]), axis=(0, 2))


def update(solution, residual, image, along, energy):
    alpha = along / (energy + epsilon)
    scale_rows = jnp.tile(alpha, 3)[:, None]
    return (solution + scale_rows * residual, residual - scale_rows * image)


def shards(rhs, blocks, owners, conn):
    groups = lax.axis_size("grp")
    held = blocks.shape[0]
    capacity = max(2, 3 * held // 8)
    send_blocks, send_links = place_blocks(blocks, owners, conn, groups, capacity)
    got_blocks, got_links = (
        lax.all_to_all(send_blocks, "grp", split_axis=0, concat_axis=0, tiled=True),
        lax.all_to_all(send_links, "grp", split_axis=0, concat_axis=0, tiled=True),
    )
    matrices = got_blocks[:, :, :6561].reshape(groups * capacity, 81, 81)
    residual = rhs
    solution = jnp.zeros(rhs.shape, jnp.float32)
    own_count = rhs.shape[1]
    band_width = 2 * held
    local_links = jnp.clip(
        got_links - lax.axis_index("sub") * own_count, 0, own_count + band_width - 1
    ).astype(jnp.int32)
    places = jnp.arange(own_count + band_width, dtype=jnp.int32)
    selector = (places[:, None] == local_links.reshape(1, -1)).astype(jnp.bfloat16)
    for step in range(STEPS):
        rounded = residual.astype(jnp.bfloat16)
        upper = passed_along(rounded[:, :band_width], "sub", -1)
        field = jnp.concatenate([rounded, upper], axis=1)
        partial_sum = element_products(matrices, selector, field)
        incoming = passed_along(partial_sum[:, own_count:], "sub", 1)
        image = partial_sum[:, :own_count] + jnp.pad(
            incoming, ((0, 0), (0, own_count - band_width))
        )
        sums = total_over_devices(
            jnp.stack([column_sums(residual, image), column_sums(image, image)]), step
        )
        along, energy = sums[0], sums[1]
        solution, residual = update(solution, residual, image, along, energy)
    return (solution, residual)


def solution(mesh):
    return jax.shard_map(
        shards,
        mesh=mesh,
        in_specs=(
            P(None, ("grp", "sub")),
            P(("grp", "sub"), None),
            P(("grp", "sub"), None),
            P(("grp", "sub"), None),
        ),
        out_specs=(P(None, ("grp", "sub")), P(None, ("grp", "sub"))),
        check_vma=False,
    )
```

```python
import functools

import jax
import jax.numpy as jnp
from jax import lax
from jax.experimental import pallas as pl
from jax.experimental.pallas import tpu as pltpu
from jax.sharding import PartitionSpec as P

MESH = pl.DeviceIdType.MESH

STEPS = 2


epsilon = 1e-06


def passed_along(block, axis, distance):
    devices = range(lax.axis_size(axis))
    route = [(i - distance, i) for i in devices if i - distance in devices]
    return lax.ppermute(block, axis, route)


def place_blocks(blocks, owners, conn, groups, capacity):
    owner_group = owners[:, 0]
    onehot = (owner_group[:, None] == jnp.arange(groups, dtype=jnp.int32)[None, :]).astype(
        jnp.int32
    )
    before = jnp.cumsum(onehot, axis=0) - onehot
    position = jnp.sum(before * onehot, axis=1)
    target = owner_group * capacity + position
    send_blocks = (
        jnp.zeros((groups * capacity, blocks.shape[1]), blocks.dtype).at[target].set(blocks)
    )
    send_links = jnp.zeros((groups * capacity, conn.shape[1]), jnp.int32).at[target].set(conn)
    return (send_blocks.reshape(groups, capacity, -1), send_links.reshape(groups, capacity, -1))


def element_products(matrices, selector, own_field, upper_field):
    rows = own_field.shape[0]
    own_count = own_field.shape[1]
    count = matrices.shape[0]
    contract = (((0,), (1,)), ((), ()))
    picked = lax.dot_general(
        selector[:own_count], own_field, contract, preferred_element_type=jnp.float32
    )
    picked = picked + lax.dot_general(
        selector[own_count:], upper_field, contract, preferred_element_type=jnp.float32
    )
    picked = picked.astype(jnp.bfloat16).reshape(count, 81, rows // 3)
    result = jnp.einsum("sab,sao->sbo", matrices, picked, preferred_element_type=jnp.float32)
    result = result.reshape(count * 27, rows)
    high_part = result.astype(jnp.bfloat16)
    low_part = (result - high_part.astype(jnp.float32)).astype(jnp.bfloat16)
    parts = jnp.concatenate([high_part, low_part], axis=1)
    halo = jnp.dot(selector[own_count:], parts, preferred_element_type=jnp.float32)
    halo = (halo[:, :rows] + halo[:, rows:]).T
    incoming = passed_along(halo, "sub", 1)
    own = jnp.dot(selector[:own_count], parts, preferred_element_type=jnp.float32)
    own = (own[:, :rows] + own[:, rows:]).T
    return own + jnp.pad(incoming, ((0, 0), (0, own_count - incoming.shape[1])))


def gather_sum_kernel(n_grp, n_sub, x_ref, o_ref, slots, send_sem, recv_sem):
    my_grp = lax.axis_index("grp")
    my_sub = lax.axis_index("sub")
    barrier = pltpu.get_barrier_semaphore()
    for d in range(1, n_sub):
        target = (my_grp, (my_sub + d) % n_sub)
        pl.semaphore_signal(barrier, inc=1, device_id=target, device_id_type=MESH)
    for d in range(1, n_grp):
        target = ((my_grp + d) % n_grp, my_sub)
        pl.semaphore_signal(barrier, inc=1, device_id=target, device_id_type=MESH)
    pl.semaphore_wait(barrier, n_sub - 1 + n_grp - 1)

    def exchange(value, first, count, my_index, device_of):
        slots[first + my_index] = value
        sends = []
        for d in range(1, count):
            copy = pltpu.make_async_remote_copy(
                src_ref=slots.at[first + my_index],
                dst_ref=slots.at[first + my_index],
                send_sem=send_sem.at[first + d],
                recv_sem=recv_sem.at[first + my_index],
                device_id=device_of((my_index + d) % count),
                device_id_type=MESH,
            )
            copy.start()
            sends.append(copy)
        for d in range(1, count):
            source = (my_index + count - d) % count
            pltpu.make_async_remote_copy(
                src_ref=slots.at[first + source],
                dst_ref=slots.at[first + source],
                send_sem=send_sem.at[first + d],
                recv_sem=recv_sem.at[first + source],
                device_id=device_of(source),
                device_id_type=MESH,
            ).wait_recv()
        for copy in sends:
            copy.wait_send()
        total = slots[first]
        for i in range(1, count):
            total = total + slots[first + i]
        return total

    partial_sum = exchange(x_ref[...], 0, n_sub, my_sub, lambda i: (my_grp, i))
    o_ref[...] = exchange(partial_sum, n_sub, n_grp, my_grp, lambda i: (i, my_sub))


def total_over_devices(value, call):
    n_grp = lax.axis_size("grp")
    n_sub = lax.axis_size("sub")
    flat = value.reshape(-1)
    block = jnp.zeros((8 * 128,), jnp.float32).at[: flat.shape[0]].set(flat)
    block = block.reshape(8, 128)
    summed = pl.pallas_call(
        functools.partial(gather_sum_kernel, n_grp, n_sub),
        out_shape=jax.ShapeDtypeStruct((8, 128), jnp.float32),
        in_specs=[pl.BlockSpec(memory_space=pltpu.VMEM)],
        out_specs=pl.BlockSpec(memory_space=pltpu.VMEM),
        scratch_shapes=[
            pltpu.VMEM((n_sub + n_grp, 8, 128), jnp.float32),
            pltpu.SemaphoreType.DMA((n_sub + n_grp,)),
            pltpu.SemaphoreType.DMA((n_sub + n_grp,)),
        ],
        compiler_params=pltpu.CompilerParams(collective_id=call, has_side_effects=True),
    )(block)
    return summed.reshape(-1)[: flat.shape[0]].reshape(value.shape)


def column_sums(first, second):
    return jnp.sum((first * second).reshape(3, -1, first.shape[1]), axis=(0, 2))


def update(solution, residual, image, along, energy):
    alpha = along / (energy + epsilon)
    scale_rows = jnp.tile(alpha, 3)[:, None]
    return (solution + scale_rows * residual, residual - scale_rows * image)


def shards(rhs, blocks, owners, conn):
    groups = lax.axis_size("grp")
    held = blocks.shape[0]
    capacity = max(2, 3 * held // 8)
    send_blocks, send_links = place_blocks(blocks, owners, conn, groups, capacity)
    got_blocks, got_links = (
        lax.all_to_all(send_blocks, "grp", split_axis=0, concat_axis=0, tiled=True),
        lax.all_to_all(send_links, "grp", split_axis=0, concat_axis=0, tiled=True),
    )
    matrices = got_blocks[:, :, :6561].reshape(groups * capacity, 81, 81)
    residual = rhs
    solution = jnp.zeros(rhs.shape, jnp.float32)
    own_count = rhs.shape[1]
    band_width = 2 * held
    local_links = jnp.clip(
        got_links - lax.axis_index("sub") * own_count, 0, own_count + band_width - 1
    ).astype(jnp.int32)
    places = jnp.arange(own_count + band_width, dtype=jnp.int32)
    selector = (places[:, None] == local_links.reshape(1, -1)).astype(jnp.bfloat16)
    for step in range(STEPS):
        rounded = residual.astype(jnp.bfloat16)
        upper = passed_along(rounded[:, :band_width], "sub", -1)
        image = element_products(matrices, selector, rounded, upper)
        sums = total_over_devices(
            jnp.stack([column_sums(residual, image), column_sums(image, image)]), step
        )
        along, energy = sums[0], sums[1]
        solution, residual = update(solution, residual, image, along, energy)
    return (solution, residual)


def solution(mesh):
    return jax.shard_map(
        shards,
        mesh=mesh,
        in_specs=(
            P(None, ("grp", "sub")),
            P(("grp", "sub"), None),
            P(("grp", "sub"), None),
            P(("grp", "sub"), None),
        ),
        out_specs=(P(None, ("grp", "sub")), P(None, ("grp", "sub"))),
        check_vma=False,
    )
```

```python
import functools

import jax
import jax.numpy as jnp
from jax import lax
from jax.experimental import pallas as pl
from jax.experimental.pallas import tpu as pltpu
from jax.sharding import PartitionSpec as P

MESH = pl.DeviceIdType.MESH

STEPS = 2


epsilon = 1e-06


def passed_along(block, axis, distance):
    devices = range(lax.axis_size(axis))
    route = [(i - distance, i) for i in devices if i - distance in devices]
    return lax.ppermute(block, axis, route)


def place_blocks(blocks, owners, conn, groups, capacity):
    owner_group = owners[:, 0]
    onehot = (owner_group[:, None] == jnp.arange(groups, dtype=jnp.int32)[None, :]).astype(
        jnp.int32
    )
    before = jnp.cumsum(onehot, axis=0) - onehot
    position = jnp.sum(before * onehot, axis=1)
    target = owner_group * capacity + position
    send_blocks = (
        jnp.zeros((groups * capacity, blocks.shape[1]), blocks.dtype).at[target].set(blocks)
    )
    send_links = jnp.zeros((groups * capacity, conn.shape[1]), jnp.int32).at[target].set(conn)
    return (send_blocks.reshape(groups, capacity, -1), send_links.reshape(groups, capacity, -1))


def element_products(matrix_parts, selector, field):
    rows = field.shape[0]
    count = sum(part.shape[0] for part in matrix_parts)
    picked = lax.dot_general(
        selector, field, (((0,), (1,)), ((), ())), preferred_element_type=jnp.float32
    ).astype(jnp.bfloat16)
    picked = picked.reshape(count, 81, rows // 3)
    results = []
    first = 0
    for part in matrix_parts:
        share = picked[first : first + part.shape[0]]
        results.append(jnp.einsum("sab,sao->sbo", part, share, preferred_element_type=jnp.float32))
        first += part.shape[0]
    result = jnp.concatenate(results, axis=0).reshape(count * 27, rows)
    high_part = result.astype(jnp.bfloat16)
    low_part = (result - high_part.astype(jnp.float32)).astype(jnp.bfloat16)
    parts = jnp.concatenate([high_part, low_part], axis=1)
    acc = jnp.dot(selector, parts, preferred_element_type=jnp.float32)
    return (acc[:, :rows] + acc[:, rows:]).T


def gather_sum_kernel(n_grp, n_sub, x_ref, o_ref, slots, send_sem, recv_sem):
    my_grp = lax.axis_index("grp")
    my_sub = lax.axis_index("sub")
    barrier = pltpu.get_barrier_semaphore()
    for d in range(1, n_sub):
        target = (my_grp, (my_sub + d) % n_sub)
        pl.semaphore_signal(barrier, inc=1, device_id=target, device_id_type=MESH)
    for d in range(1, n_grp):
        target = ((my_grp + d) % n_grp, my_sub)
        pl.semaphore_signal(barrier, inc=1, device_id=target, device_id_type=MESH)
    pl.semaphore_wait(barrier, n_sub - 1 + n_grp - 1)

    def exchange(value, first, count, my_index, device_of):
        slots[first + my_index] = value
        sends = []
        for d in range(1, count):
            copy = pltpu.make_async_remote_copy(
                src_ref=slots.at[first + my_index],
                dst_ref=slots.at[first + my_index],
                send_sem=send_sem.at[first + d],
                recv_sem=recv_sem.at[first + my_index],
                device_id=device_of((my_index + d) % count),
                device_id_type=MESH,
            )
            copy.start()
            sends.append(copy)
        for d in range(1, count):
            source = (my_index + count - d) % count
            pltpu.make_async_remote_copy(
                src_ref=slots.at[first + source],
                dst_ref=slots.at[first + source],
                send_sem=send_sem.at[first + d],
                recv_sem=recv_sem.at[first + source],
                device_id=device_of(source),
                device_id_type=MESH,
            ).wait_recv()
        for copy in sends:
            copy.wait_send()
        total = slots[first]
        for i in range(1, count):
            total = total + slots[first + i]
        return total

    partial_sum = exchange(x_ref[...], 0, n_sub, my_sub, lambda i: (my_grp, i))
    o_ref[...] = exchange(partial_sum, n_sub, n_grp, my_grp, lambda i: (i, my_sub))


def total_over_devices(value, call):
    n_grp = lax.axis_size("grp")
    n_sub = lax.axis_size("sub")
    flat = value.reshape(-1)
    block = jnp.zeros((8 * 128,), jnp.float32).at[: flat.shape[0]].set(flat)
    block = block.reshape(8, 128)
    summed = pl.pallas_call(
        functools.partial(gather_sum_kernel, n_grp, n_sub),
        out_shape=jax.ShapeDtypeStruct((8, 128), jnp.float32),
        in_specs=[pl.BlockSpec(memory_space=pltpu.VMEM)],
        out_specs=pl.BlockSpec(memory_space=pltpu.VMEM),
        scratch_shapes=[
            pltpu.VMEM((n_sub + n_grp, 8, 128), jnp.float32),
            pltpu.SemaphoreType.DMA((n_sub + n_grp,)),
            pltpu.SemaphoreType.DMA((n_sub + n_grp,)),
        ],
        compiler_params=pltpu.CompilerParams(collective_id=call, has_side_effects=True),
    )(block)
    return summed.reshape(-1)[: flat.shape[0]].reshape(value.shape)


def column_sums(first, second):
    return jnp.sum((first * second).reshape(3, -1, first.shape[1]), axis=(0, 2))


def update(solution, residual, image, along, energy):
    alpha = along / (energy + epsilon)
    scale_rows = jnp.tile(alpha, 3)[:, None]
    return (solution + scale_rows * residual, residual - scale_rows * image)


def shards(rhs, blocks, owners, conn):
    groups = lax.axis_size("grp")
    held = blocks.shape[0]
    capacity = max(2, 3 * held // 8)
    send_blocks, send_links = place_blocks(blocks, owners, conn, groups, capacity)
    my_column = lax.axis_index("grp")
    got_links = lax.all_to_all(send_links, "grp", split_axis=0, concat_axis=0, tiled=True)
    matrix_parts = []
    link_parts = []
    for d in range(groups):
        outgoing = lax.dynamic_index_in_dim(send_blocks, (my_column + d) % groups, 0, False)
        if d:
            route = [(g, (g + d) % groups) for g in range(groups)]
            outgoing = lax.ppermute(outgoing, "grp", route)
        matrix_parts.append(outgoing[:, :6561].reshape(capacity, 81, 81))
        source = (my_column + groups - d) % groups
        link_parts.append(lax.dynamic_index_in_dim(got_links, source, 0, False))
    got_links = jnp.stack(link_parts)
    residual = rhs
    solution = jnp.zeros(rhs.shape, jnp.float32)
    own_count = rhs.shape[1]
    band_width = 2 * held
    local_links = jnp.clip(
        got_links - lax.axis_index("sub") * own_count, 0, own_count + band_width - 1
    ).astype(jnp.int32)
    places = jnp.arange(own_count + band_width, dtype=jnp.int32)
    selector = (places[:, None] == local_links.reshape(1, -1)).astype(jnp.bfloat16)
    for step in range(STEPS):
        rounded = residual.astype(jnp.bfloat16)
        upper = passed_along(rounded[:, :band_width], "sub", -1)
        field = jnp.concatenate([rounded, upper], axis=1)
        partial_sum = element_products(matrix_parts, selector, field)
        incoming = passed_along(partial_sum[:, own_count:], "sub", 1)
        image = partial_sum[:, :own_count] + jnp.pad(
            incoming, ((0, 0), (0, own_count - band_width))
        )
        sums = total_over_devices(
            jnp.stack([column_sums(residual, image), column_sums(image, image)]), step
        )
        along, energy = sums[0], sums[1]
        solution, residual = update(solution, residual, image, along, energy)
    return (solution, residual)


def solution(mesh):
    return jax.shard_map(
        shards,
        mesh=mesh,
        in_specs=(
            P(None, ("grp", "sub")),
            P(("grp", "sub"), None),
            P(("grp", "sub"), None),
            P(("grp", "sub"), None),
        ),
        out_specs=(P(None, ("grp", "sub")), P(None, ("grp", "sub"))),
        check_vma=False,
    )
```

```python
import functools

import jax
import jax.numpy as jnp
from jax import lax
from jax.experimental import pallas as pl
from jax.experimental.pallas import tpu as pltpu
from jax.sharding import PartitionSpec as P

MESH = pl.DeviceIdType.MESH

STEPS = 2


epsilon = 1e-06


def passed_along(block, axis, distance):
    devices = range(lax.axis_size(axis))
    route = [(i - distance, i) for i in devices if i - distance in devices]
    return lax.ppermute(block, axis, route)


def place_blocks(blocks, owners, conn, groups, capacity):
    owner_group = owners[:, 0]
    onehot = (owner_group[:, None] == jnp.arange(groups, dtype=jnp.int32)[None, :]).astype(
        jnp.int32
    )
    before = jnp.cumsum(onehot, axis=0) - onehot
    position = jnp.sum(before * onehot, axis=1)
    target = owner_group * capacity + position
    send_blocks = (
        jnp.zeros((groups * capacity, blocks.shape[1]), blocks.dtype).at[target].set(blocks)
    )
    send_links = jnp.zeros((groups * capacity, conn.shape[1]), jnp.int32).at[target].set(conn)
    return (send_blocks.reshape(groups, capacity, -1), send_links.reshape(groups, capacity, -1))


def element_products(matrices, selector, own_field, upper_field, split):
    rows = own_field.shape[0]
    own_count = own_field.shape[1]
    count = matrices.shape[0]
    contract = (((0,), (1,)), ((), ()))
    if split is not None:
        links = split
        own_places = jnp.arange(own_count, dtype=jnp.int32)
        upper_places = jnp.arange(upper_field.shape[1], dtype=jnp.int32) + own_count
        own_selector = (own_places[:, None] == links).astype(jnp.bfloat16)
        upper_selector = (upper_places[:, None] == links).astype(jnp.bfloat16)
        picked = lax.dot_general(
            own_selector, own_field, contract, preferred_element_type=jnp.float32
        )
        picked = picked + lax.dot_general(
            upper_selector, upper_field, contract, preferred_element_type=jnp.float32
        )
    else:
        field = jnp.concatenate([own_field, upper_field], axis=1)
        picked = lax.dot_general(selector, field, contract, preferred_element_type=jnp.float32)
    picked = picked.astype(jnp.bfloat16)
    picked = picked.reshape(count, 81, rows // 3)
    result = jnp.einsum("sab,sao->sbo", matrices, picked, preferred_element_type=jnp.float32)
    result = result.reshape(count * 27, rows)
    high_part = result.astype(jnp.bfloat16)
    low_part = (result - high_part.astype(jnp.float32)).astype(jnp.bfloat16)
    parts = jnp.concatenate([high_part, low_part], axis=1)
    acc = jnp.dot(selector, parts, preferred_element_type=jnp.float32)
    return (acc[:, :rows] + acc[:, rows:]).T


def gather_sum_kernel(n_grp, n_sub, x_ref, o_ref, slots, send_sem, recv_sem):
    my_grp = lax.axis_index("grp")
    my_sub = lax.axis_index("sub")
    barrier = pltpu.get_barrier_semaphore()
    for d in range(1, n_sub):
        target = (my_grp, (my_sub + d) % n_sub)
        pl.semaphore_signal(barrier, inc=1, device_id=target, device_id_type=MESH)
    for d in range(1, n_grp):
        target = ((my_grp + d) % n_grp, my_sub)
        pl.semaphore_signal(barrier, inc=1, device_id=target, device_id_type=MESH)
    pl.semaphore_wait(barrier, n_sub - 1 + n_grp - 1)

    def exchange(value, first, count, my_index, device_of):
        slots[first + my_index] = value
        sends = []
        for d in range(1, count):
            copy = pltpu.make_async_remote_copy(
                src_ref=slots.at[first + my_index],
                dst_ref=slots.at[first + my_index],
                send_sem=send_sem.at[first + d],
                recv_sem=recv_sem.at[first + my_index],
                device_id=device_of((my_index + d) % count),
                device_id_type=MESH,
            )
            copy.start()
            sends.append(copy)
        for d in range(1, count):
            source = (my_index + count - d) % count
            pltpu.make_async_remote_copy(
                src_ref=slots.at[first + source],
                dst_ref=slots.at[first + source],
                send_sem=send_sem.at[first + d],
                recv_sem=recv_sem.at[first + source],
                device_id=device_of(source),
                device_id_type=MESH,
            ).wait_recv()
        for copy in sends:
            copy.wait_send()
        total = slots[first]
        for i in range(1, count):
            total = total + slots[first + i]
        return total

    partial_sum = exchange(x_ref[...], 0, n_sub, my_sub, lambda i: (my_grp, i))
    o_ref[...] = exchange(partial_sum, n_sub, n_grp, my_grp, lambda i: (i, my_sub))


def total_over_devices(value, call):
    n_grp = lax.axis_size("grp")
    n_sub = lax.axis_size("sub")
    flat = value.reshape(-1)
    block = jnp.zeros((8 * 128,), jnp.float32).at[: flat.shape[0]].set(flat)
    block = block.reshape(8, 128)
    summed = pl.pallas_call(
        functools.partial(gather_sum_kernel, n_grp, n_sub),
        out_shape=jax.ShapeDtypeStruct((8, 128), jnp.float32),
        in_specs=[pl.BlockSpec(memory_space=pltpu.VMEM)],
        out_specs=pl.BlockSpec(memory_space=pltpu.VMEM),
        scratch_shapes=[
            pltpu.VMEM((n_sub + n_grp, 8, 128), jnp.float32),
            pltpu.SemaphoreType.DMA((n_sub + n_grp,)),
            pltpu.SemaphoreType.DMA((n_sub + n_grp,)),
        ],
        compiler_params=pltpu.CompilerParams(collective_id=call, has_side_effects=True),
    )(block)
    return summed.reshape(-1)[: flat.shape[0]].reshape(value.shape)


def column_sums(first, second):
    return jnp.sum((first * second).reshape(3, -1, first.shape[1]), axis=(0, 2))


def update(solution, residual, image, along, energy):
    alpha = along / (energy + epsilon)
    scale_rows = jnp.tile(alpha, 3)[:, None]
    return (solution + scale_rows * residual, residual - scale_rows * image)


def shards(rhs, blocks, owners, conn):
    groups = lax.axis_size("grp")
    held = blocks.shape[0]
    capacity = max(2, 3 * held // 8)
    send_blocks, send_links = place_blocks(blocks, owners, conn, groups, capacity)
    got_blocks, got_links = (
        lax.all_to_all(send_blocks, "grp", split_axis=0, concat_axis=0, tiled=True),
        lax.all_to_all(send_links, "grp", split_axis=0, concat_axis=0, tiled=True),
    )
    matrices = got_blocks[:, :, :6561].reshape(groups * capacity, 81, 81)
    residual = rhs
    solution = jnp.zeros(rhs.shape, jnp.float32)
    own_count = rhs.shape[1]
    band_width = 2 * held
    local_links = jnp.clip(
        got_links - lax.axis_index("sub") * own_count, 0, own_count + band_width - 1
    ).astype(jnp.int32)
    places = jnp.arange(own_count + band_width, dtype=jnp.int32)
    selector = (places[:, None] == local_links.reshape(1, -1)).astype(jnp.bfloat16)
    for step in range(STEPS):
        rounded = residual.astype(jnp.bfloat16)
        upper = passed_along(rounded[:, :band_width], "sub", -1)
        split = local_links.reshape(1, -1) if step else None
        partial_sum = element_products(matrices, selector, rounded, upper, split)
        incoming = passed_along(partial_sum[:, own_count:], "sub", 1)
        image = partial_sum[:, :own_count] + jnp.pad(
            incoming, ((0, 0), (0, own_count - band_width))
        )
        sums = total_over_devices(
            jnp.stack([column_sums(residual, image), column_sums(image, image)]), step
        )
        along, energy = sums[0], sums[1]
        solution, residual = update(solution, residual, image, along, energy)
    return (solution, residual)


def solution(mesh):
    return jax.shard_map(
        shards,
        mesh=mesh,
        in_specs=(
            P(None, ("grp", "sub")),
            P(("grp", "sub"), None),
            P(("grp", "sub"), None),
            P(("grp", "sub"), None),
        ),
        out_specs=(P(None, ("grp", "sub")), P(None, ("grp", "sub"))),
        check_vma=False,
    )
```

```python
import functools

import jax
import jax.numpy as jnp
from jax import lax
from jax.experimental import pallas as pl
from jax.experimental.pallas import tpu as pltpu
from jax.sharding import PartitionSpec as P

MESH = pl.DeviceIdType.MESH

STEPS = 2


epsilon = 1e-06


def passed_along(block, axis, distance):
    devices = range(lax.axis_size(axis))
    route = [(i - distance, i) for i in devices if i - distance in devices]
    return lax.ppermute(block, axis, route)


def place_blocks(blocks, owners, conn, groups, capacity):
    owner_group = owners[:, 0]
    onehot = (owner_group[:, None] == jnp.arange(groups, dtype=jnp.int32)[None, :]).astype(
        jnp.int32
    )
    before = jnp.cumsum(onehot, axis=0) - onehot
    position = jnp.sum(before * onehot, axis=1)
    target = owner_group * capacity + position
    send_blocks = (
        jnp.zeros((groups * capacity, blocks.shape[1]), blocks.dtype).at[target].set(blocks)
    )
    send_links = jnp.zeros((groups * capacity, conn.shape[1]), jnp.int32).at[target].set(conn)
    return (send_blocks.reshape(groups, capacity, -1), send_links.reshape(groups, capacity, -1))


def element_products(matrices, selector, own_field, upper_field, split):
    rows = own_field.shape[0]
    own_count = own_field.shape[1]
    count = matrices.shape[0]
    contract = (((0,), (1,)), ((), ()))
    if split is not None:
        links = split
        own_places = jnp.arange(own_count, dtype=jnp.int32)
        upper_places = jnp.arange(upper_field.shape[1], dtype=jnp.int32) + own_count
        own_selector = (own_places[:, None] == links).astype(jnp.bfloat16)
        upper_selector = (upper_places[:, None] == links).astype(jnp.bfloat16)
        picked = lax.dot_general(
            own_selector, own_field, contract, preferred_element_type=jnp.float32
        )
        picked = picked + lax.dot_general(
            upper_selector, upper_field, contract, preferred_element_type=jnp.float32
        )
    else:
        field = jnp.concatenate([own_field, upper_field], axis=1)
        picked = lax.dot_general(selector, field, contract, preferred_element_type=jnp.float32)
    picked = picked.astype(jnp.bfloat16)
    picked = picked.reshape(count, 81, rows // 3)
    result = jnp.einsum("sab,sao->sbo", matrices, picked, preferred_element_type=jnp.float32)
    result = result.reshape(count * 27, rows)
    high_part = result.astype(jnp.bfloat16)
    low_part = (result - high_part.astype(jnp.float32)).astype(jnp.bfloat16)
    parts = jnp.concatenate([high_part, low_part], axis=1)
    acc = jnp.dot(selector, parts, preferred_element_type=jnp.float32)
    return (acc[:, :rows] + acc[:, rows:]).T


def image_sums_kernel(
    n_grp, n_sub, res_ref, part_ref, image_ref, sums_ref,
    halo, slots, send_sem, recv_sem, halo_send, halo_recv,
):
    my_grp = lax.axis_index("grp")
    my_sub = lax.axis_index("sub")
    own_count = image_ref.shape[1]
    band = halo.shape[1]
    rows = res_ref.shape[0]
    barrier = pltpu.get_barrier_semaphore()
    for d in range(1, n_sub):
        target = (my_grp, (my_sub + d) % n_sub)
        pl.semaphore_signal(barrier, inc=1, device_id=target, device_id_type=MESH)
    for d in range(1, n_grp):
        target = ((my_grp + d) % n_grp, my_sub)
        pl.semaphore_signal(barrier, inc=1, device_id=target, device_id_type=MESH)
    pl.semaphore_wait(barrier, n_sub - 1 + n_grp - 1)

    def halo_copy(target_sub):
        return pltpu.make_async_remote_copy(
            src_ref=part_ref.at[:, pl.ds(own_count, band)],
            dst_ref=halo,
            send_sem=halo_send,
            recv_sem=halo_recv,
            device_id=(my_grp, target_sub),
            device_id_type=MESH,
        )

    @pl.when(my_sub < n_sub - 1)
    def _():
        halo_copy(my_sub + 1).start()

    image_ref[...] = part_ref[:, pl.ds(0, own_count)]

    @pl.when(my_sub > 0)
    def _():
        halo_copy(my_sub - 1).wait_recv()
        image_ref[:, pl.ds(0, band)] = image_ref[:, pl.ds(0, band)] + halo[...]

    @pl.when(my_sub < n_sub - 1)
    def _():
        halo_copy(my_sub + 1).wait_send()

    image = image_ref[...]
    residual = res_ref[...]
    along = jnp.sum(residual * image, axis=1, keepdims=True)
    energy = jnp.sum(image * image, axis=1, keepdims=True)
    width = rows // 3
    along = along[0:width] + along[width : 2 * width] + along[2 * width :]
    energy = energy[0:width] + energy[width : 2 * width] + energy[2 * width :]
    lane = lax.broadcasted_iota(jnp.int32, (width, 128), 1)
    block = jnp.where(lane == 0, along, jnp.where(lane == 1, energy, 0.0))

    def exchange(value, first, count, my_index, device_of):
        slots[first + my_index] = value
        sends = []
        for d in range(1, count):
            copy = pltpu.make_async_remote_copy(
                src_ref=slots.at[first + my_index],
                dst_ref=slots.at[first + my_index],
                send_sem=send_sem.at[first + d],
                recv_sem=recv_sem.at[first + my_index],
                device_id=device_of((my_index + d) % count),
                device_id_type=MESH,
            )
            copy.start()
            sends.append(copy)
        for d in range(1, count):
            source = (my_index + count - d) % count
            pltpu.make_async_remote_copy(
                src_ref=slots.at[first + source],
                dst_ref=slots.at[first + source],
                send_sem=send_sem.at[first + d],
                recv_sem=recv_sem.at[first + source],
                device_id=device_of(source),
                device_id_type=MESH,
            ).wait_recv()
        for copy in sends:
            copy.wait_send()
        total = slots[first]
        for i in range(1, count):
            total = total + slots[first + i]
        return total

    partial_sum = exchange(block, 0, n_sub, my_sub, lambda i: (my_grp, i))
    sums_ref[...] = exchange(partial_sum, n_sub, n_grp, my_grp, lambda i: (i, my_sub))


def image_and_sums(residual, partial_sum, call):
    n_grp = lax.axis_size("grp")
    n_sub = lax.axis_size("sub")
    rows, own_count = residual.shape
    band = partial_sum.shape[1] - own_count
    width = rows // 3
    image, sums = pl.pallas_call(
        functools.partial(image_sums_kernel, n_grp, n_sub),
        out_shape=(
            jax.ShapeDtypeStruct((rows, own_count), jnp.float32),
            jax.ShapeDtypeStruct((width, 128), jnp.float32),
        ),
        in_specs=[pl.BlockSpec(memory_space=pltpu.VMEM)] * 2,
        out_specs=(pl.BlockSpec(memory_space=pltpu.VMEM),) * 2,
        scratch_shapes=[
            pltpu.VMEM((rows, band), jnp.float32),
            pltpu.VMEM((n_sub + n_grp, width, 128), jnp.float32),
            pltpu.SemaphoreType.DMA((n_sub + n_grp,)),
            pltpu.SemaphoreType.DMA((n_sub + n_grp,)),
            pltpu.SemaphoreType.DMA(()),
            pltpu.SemaphoreType.DMA(()),
        ],
        compiler_params=pltpu.CompilerParams(collective_id=call, has_side_effects=True),
    )(residual, partial_sum)
    return image, sums[:, 0], sums[:, 1]


def column_sums(first, second):
    return jnp.sum((first * second).reshape(3, -1, first.shape[1]), axis=(0, 2))


def update(solution, residual, image, along, energy):
    alpha = along / (energy + epsilon)
    scale_rows = jnp.tile(alpha, 3)[:, None]
    return (solution + scale_rows * residual, residual - scale_rows * image)


def shards(rhs, blocks, owners, conn):
    groups = lax.axis_size("grp")
    held = blocks.shape[0]
    capacity = max(2, 3 * held // 8)
    send_blocks, send_links = place_blocks(blocks, owners, conn, groups, capacity)
    got_blocks, got_links = (
        lax.all_to_all(send_blocks, "grp", split_axis=0, concat_axis=0, tiled=True),
        lax.all_to_all(send_links, "grp", split_axis=0, concat_axis=0, tiled=True),
    )
    matrices = got_blocks[:, :, :6561].reshape(groups * capacity, 81, 81)
    residual = rhs
    solution = jnp.zeros(rhs.shape, jnp.float32)
    own_count = rhs.shape[1]
    band_width = 2 * held
    local_links = jnp.clip(
        got_links - lax.axis_index("sub") * own_count, 0, own_count + band_width - 1
    ).astype(jnp.int32)
    places = jnp.arange(own_count + band_width, dtype=jnp.int32)
    selector = (places[:, None] == local_links.reshape(1, -1)).astype(jnp.bfloat16)
    for step in range(STEPS):
        rounded = residual.astype(jnp.bfloat16)
        upper = passed_along(rounded[:, :band_width], "sub", -1)
        split = local_links.reshape(1, -1) if step else None
        partial_sum = element_products(matrices, selector, rounded, upper, split)
        image, along, energy = image_and_sums(residual, partial_sum, step)
        solution, residual = update(solution, residual, image, along, energy)
    return (solution, residual)


def solution(mesh):
    return jax.shard_map(
        shards,
        mesh=mesh,
        in_specs=(
            P(None, ("grp", "sub")),
            P(("grp", "sub"), None),
            P(("grp", "sub"), None),
            P(("grp", "sub"), None),
        ),
        out_specs=(P(None, ("grp", "sub")), P(None, ("grp", "sub"))),
        check_vma=False,
    )
```

```python
import functools

import jax
import jax.numpy as jnp
from jax import lax
from jax.experimental import pallas as pl
from jax.experimental.pallas import tpu as pltpu
from jax.sharding import PartitionSpec as P

MESH = pl.DeviceIdType.MESH

STEPS = 2


epsilon = 1e-06


def passed_along(block, axis, distance):
    devices = range(lax.axis_size(axis))
    route = [(i - distance, i) for i in devices if i - distance in devices]
    return lax.ppermute(block, axis, route)


def place_blocks(blocks, owners, conn, groups, capacity):
    owner_group = owners[:, 0]
    onehot = (owner_group[:, None] == jnp.arange(groups, dtype=jnp.int32)[None, :]).astype(
        jnp.int32
    )
    before = jnp.cumsum(onehot, axis=0) - onehot
    position = jnp.sum(before * onehot, axis=1)
    target = owner_group * capacity + position
    send_blocks = (
        jnp.zeros((groups * capacity, blocks.shape[1]), blocks.dtype).at[target].set(blocks)
    )
    send_links = jnp.zeros((groups * capacity, conn.shape[1]), jnp.int32).at[target].set(conn)
    return (send_blocks.reshape(groups, capacity, -1), send_links.reshape(groups, capacity, -1))


def element_products(matrices, selector, own_field, upper_field, split):
    rows = own_field.shape[0]
    own_count = own_field.shape[1]
    count = matrices.shape[0]
    contract = (((0,), (1,)), ((), ()))
    if split is not None:
        links = split
        own_places = jnp.arange(own_count, dtype=jnp.int32)
        upper_places = jnp.arange(upper_field.shape[1], dtype=jnp.int32) + own_count
        own_selector = (own_places[:, None] == links).astype(jnp.bfloat16)
        upper_selector = (upper_places[:, None] == links).astype(jnp.bfloat16)
        picked = lax.dot_general(
            own_selector, own_field, contract, preferred_element_type=jnp.float32
        )
        picked = picked + lax.dot_general(
            upper_selector, upper_field, contract, preferred_element_type=jnp.float32
        )
    else:
        field = jnp.concatenate([own_field, upper_field], axis=1)
        picked = lax.dot_general(selector, field, contract, preferred_element_type=jnp.float32)
    picked = picked.astype(jnp.bfloat16)
    picked = picked.reshape(count, 81, rows // 3)
    result = jnp.einsum("sab,sao->sbo", matrices, picked, preferred_element_type=jnp.float32)
    result = result.reshape(count * 27, rows)
    high_part = result.astype(jnp.bfloat16)
    low_part = (result - high_part.astype(jnp.float32)).astype(jnp.bfloat16)
    parts = jnp.concatenate([high_part, low_part], axis=1)
    acc = jnp.dot(selector, parts, preferred_element_type=jnp.float32)
    return (acc[:, :rows] + acc[:, rows:]).T


def image_sums_kernel(
    n_grp, n_sub, res_ref, part_ref, image_ref, sums_ref,
    halo, slots, send_sem, recv_sem, halo_send, halo_recv,
):
    my_grp = lax.axis_index("grp")
    my_sub = lax.axis_index("sub")
    own_count = image_ref.shape[1]
    band = halo.shape[1]
    rows = res_ref.shape[0]
    barrier = pltpu.get_barrier_semaphore()
    for d in range(1, n_sub):
        target = (my_grp, (my_sub + d) % n_sub)
        pl.semaphore_signal(barrier, inc=1, device_id=target, device_id_type=MESH)
    for d in range(1, n_grp):
        target = ((my_grp + d) % n_grp, my_sub)
        pl.semaphore_signal(barrier, inc=1, device_id=target, device_id_type=MESH)
    image_ref[...] = part_ref[:, pl.ds(0, own_count)]
    rest = own_count - band
    residual_rest = res_ref[:, pl.ds(band, rest)]
    image_rest = image_ref[:, pl.ds(band, rest)]
    along_rest = jnp.sum(residual_rest * image_rest, axis=1, keepdims=True)
    energy_rest = jnp.sum(image_rest * image_rest, axis=1, keepdims=True)
    pl.semaphore_wait(barrier, n_sub - 1 + n_grp - 1)

    def halo_copy(target_sub):
        return pltpu.make_async_remote_copy(
            src_ref=part_ref.at[:, pl.ds(own_count, band)],
            dst_ref=halo,
            send_sem=halo_send,
            recv_sem=halo_recv,
            device_id=(my_grp, target_sub),
            device_id_type=MESH,
        )

    @pl.when(my_sub < n_sub - 1)
    def _():
        halo_copy(my_sub + 1).start()

    @pl.when(my_sub > 0)
    def _():
        halo_copy(my_sub - 1).wait_recv()
        image_ref[:, pl.ds(0, band)] = image_ref[:, pl.ds(0, band)] + halo[...]

    residual_head = res_ref[:, pl.ds(0, band)]
    image_head = image_ref[:, pl.ds(0, band)]
    along = along_rest + jnp.sum(residual_head * image_head, axis=1, keepdims=True)
    energy = energy_rest + jnp.sum(image_head * image_head, axis=1, keepdims=True)

    @pl.when(my_sub < n_sub - 1)
    def _():
        halo_copy(my_sub + 1).wait_send()

    width = rows // 3
    along = along[0:width] + along[width : 2 * width] + along[2 * width :]
    energy = energy[0:width] + energy[width : 2 * width] + energy[2 * width :]
    lane = lax.broadcasted_iota(jnp.int32, (width, 128), 1)
    block = jnp.where(lane == 0, along, jnp.where(lane == 1, energy, 0.0))

    def exchange(value, first, count, my_index, device_of):
        slots[first + my_index] = value
        sends = []
        for d in range(1, count):
            copy = pltpu.make_async_remote_copy(
                src_ref=slots.at[first + my_index],
                dst_ref=slots.at[first + my_index],
                send_sem=send_sem.at[first + d],
                recv_sem=recv_sem.at[first + my_index],
                device_id=device_of((my_index + d) % count),
                device_id_type=MESH,
            )
            copy.start()
            sends.append(copy)
        for d in range(1, count):
            source = (my_index + count - d) % count
            pltpu.make_async_remote_copy(
                src_ref=slots.at[first + source],
                dst_ref=slots.at[first + source],
                send_sem=send_sem.at[first + d],
                recv_sem=recv_sem.at[first + source],
                device_id=device_of(source),
                device_id_type=MESH,
            ).wait_recv()
        for copy in sends:
            copy.wait_send()
        total = slots[first]
        for i in range(1, count):
            total = total + slots[first + i]
        return total

    partial_sum = exchange(block, 0, n_sub, my_sub, lambda i: (my_grp, i))
    sums_ref[...] = exchange(partial_sum, n_sub, n_grp, my_grp, lambda i: (i, my_sub))


def image_and_sums(residual, partial_sum, call):
    n_grp = lax.axis_size("grp")
    n_sub = lax.axis_size("sub")
    rows, own_count = residual.shape
    band = partial_sum.shape[1] - own_count
    width = rows // 3
    image, sums = pl.pallas_call(
        functools.partial(image_sums_kernel, n_grp, n_sub),
        out_shape=(
            jax.ShapeDtypeStruct((rows, own_count), jnp.float32),
            jax.ShapeDtypeStruct((width, 128), jnp.float32),
        ),
        in_specs=[pl.BlockSpec(memory_space=pltpu.VMEM)] * 2,
        out_specs=(pl.BlockSpec(memory_space=pltpu.VMEM),) * 2,
        scratch_shapes=[
            pltpu.VMEM((rows, band), jnp.float32),
            pltpu.VMEM((n_sub + n_grp, width, 128), jnp.float32),
            pltpu.SemaphoreType.DMA((n_sub + n_grp,)),
            pltpu.SemaphoreType.DMA((n_sub + n_grp,)),
            pltpu.SemaphoreType.DMA(()),
            pltpu.SemaphoreType.DMA(()),
        ],
        compiler_params=pltpu.CompilerParams(collective_id=call, has_side_effects=True),
    )(residual, partial_sum)
    return image, sums[:, 0], sums[:, 1]


def column_sums(first, second):
    return jnp.sum((first * second).reshape(3, -1, first.shape[1]), axis=(0, 2))


def update(solution, residual, image, along, energy):
    alpha = along / (energy + epsilon)
    scale_rows = jnp.tile(alpha, 3)[:, None]
    return (solution + scale_rows * residual, residual - scale_rows * image)


def shards(rhs, blocks, owners, conn):
    groups = lax.axis_size("grp")
    held = blocks.shape[0]
    capacity = max(2, 3 * held // 8)
    send_blocks, send_links = place_blocks(blocks, owners, conn, groups, capacity)
    got_blocks, got_links = (
        lax.all_to_all(send_blocks, "grp", split_axis=0, concat_axis=0, tiled=True),
        lax.all_to_all(send_links, "grp", split_axis=0, concat_axis=0, tiled=True),
    )
    matrices = got_blocks[:, :, :6561].reshape(groups * capacity, 81, 81)
    residual = rhs
    solution = jnp.zeros(rhs.shape, jnp.float32)
    own_count = rhs.shape[1]
    band_width = 2 * held
    local_links = jnp.clip(
        got_links - lax.axis_index("sub") * own_count, 0, own_count + band_width - 1
    ).astype(jnp.int32)
    places = jnp.arange(own_count + band_width, dtype=jnp.int32)
    selector = (places[:, None] == local_links.reshape(1, -1)).astype(jnp.bfloat16)
    for step in range(STEPS):
        rounded = residual.astype(jnp.bfloat16)
        upper = passed_along(rounded[:, :band_width], "sub", -1)
        split = local_links.reshape(1, -1) if step else None
        partial_sum = element_products(matrices, selector, rounded, upper, split)
        image, along, energy = image_and_sums(residual, partial_sum, step)
        solution, residual = update(solution, residual, image, along, energy)
    return (solution, residual)


def solution(mesh):
    return jax.shard_map(
        shards,
        mesh=mesh,
        in_specs=(
            P(None, ("grp", "sub")),
            P(("grp", "sub"), None),
            P(("grp", "sub"), None),
            P(("grp", "sub"), None),
        ),
        out_specs=(P(None, ("grp", "sub")), P(None, ("grp", "sub"))),
        check_vma=False,
    )
```

```python
import functools

import jax
import jax.numpy as jnp
from jax import lax
from jax.experimental import pallas as pl
from jax.experimental.pallas import tpu as pltpu
from jax.sharding import PartitionSpec as P

MESH = pl.DeviceIdType.MESH

STEPS = 2


epsilon = 1e-06


def passed_along(block, axis, distance):
    devices = range(lax.axis_size(axis))
    route = [(i - distance, i) for i in devices if i - distance in devices]
    return lax.ppermute(block, axis, route)


def place_blocks(blocks, owners, conn, groups, capacity):
    owner_group = owners[:, 0]
    onehot = (owner_group[:, None] == jnp.arange(groups, dtype=jnp.int32)[None, :]).astype(
        jnp.int32
    )
    before = jnp.cumsum(onehot, axis=0) - onehot
    position = jnp.sum(before * onehot, axis=1)
    target = owner_group * capacity + position
    send_blocks = (
        jnp.zeros((groups * capacity, blocks.shape[1]), blocks.dtype).at[target].set(blocks)
    )
    send_links = jnp.zeros((groups * capacity, conn.shape[1]), jnp.int32).at[target].set(conn)
    return (send_blocks.reshape(groups, capacity, -1), send_links.reshape(groups, capacity, -1))


def element_products(matrices, selector, own_field, upper_field, split):
    rows = own_field.shape[0]
    own_count = own_field.shape[1]
    count = matrices.shape[0]
    contract = (((0,), (1,)), ((), ()))
    if split is not None:
        links = split
        own_places = jnp.arange(own_count, dtype=jnp.int32)
        upper_places = jnp.arange(upper_field.shape[1], dtype=jnp.int32) + own_count
        own_selector = (own_places[:, None] == links).astype(jnp.bfloat16)
        upper_selector = (upper_places[:, None] == links).astype(jnp.bfloat16)
        picked = lax.dot_general(
            own_selector, own_field, contract, preferred_element_type=jnp.float32
        )
        picked = picked + lax.dot_general(
            upper_selector, upper_field, contract, preferred_element_type=jnp.float32
        )
    else:
        field = jnp.concatenate([own_field, upper_field], axis=1)
        picked = lax.dot_general(selector, field, contract, preferred_element_type=jnp.float32)
    picked = picked.astype(jnp.bfloat16)
    picked = picked.reshape(count, 81, rows // 3)
    result = jnp.einsum("sab,sao->sbo", matrices, picked, preferred_element_type=jnp.float32)
    result = result.reshape(count * 27, rows)
    high_part = result.astype(jnp.bfloat16)
    low_part = (result - high_part.astype(jnp.float32)).astype(jnp.bfloat16)
    parts = jnp.concatenate([high_part, low_part], axis=1)
    acc = jnp.dot(selector, parts, preferred_element_type=jnp.float32)
    return (acc[:, :rows] + acc[:, rows:]).T


def image_sums_kernel(
    n_grp, n_sub, res_ref, part_ref, image_ref, sums_ref,
    halo, slots, send_sem, recv_sem, halo_send, halo_recv,
):
    my_grp = lax.axis_index("grp")
    my_sub = lax.axis_index("sub")
    own_count = image_ref.shape[1]
    band = halo.shape[1]
    rows = res_ref.shape[0]
    barrier = pltpu.get_barrier_semaphore()
    for d in range(1, n_sub):
        target = (my_grp, (my_sub + d) % n_sub)
        pl.semaphore_signal(barrier, inc=1, device_id=target, device_id_type=MESH)
    for d in range(1, n_grp):
        target = ((my_grp + d) % n_grp, my_sub)
        pl.semaphore_signal(barrier, inc=1, device_id=target, device_id_type=MESH)
    image_ref[...] = part_ref[:, pl.ds(0, own_count)]
    rest = own_count - band
    residual_rest = res_ref[:, pl.ds(band, rest)]
    image_rest = image_ref[:, pl.ds(band, rest)]
    along_rest = jnp.sum(residual_rest * image_rest, axis=1, keepdims=True)
    energy_rest = jnp.sum(image_rest * image_rest, axis=1, keepdims=True)
    pl.semaphore_wait(barrier, n_sub - 1 + n_grp - 1)

    def halo_copy(target_sub):
        return pltpu.make_async_remote_copy(
            src_ref=part_ref.at[:, pl.ds(own_count, band)],
            dst_ref=halo,
            send_sem=halo_send,
            recv_sem=halo_recv,
            device_id=(my_grp, target_sub),
            device_id_type=MESH,
        )

    @pl.when(my_sub < n_sub - 1)
    def _():
        halo_copy(my_sub + 1).start()

    @pl.when(my_sub > 0)
    def _():
        halo_copy(my_sub - 1).wait_recv()
        image_ref[:, pl.ds(0, band)] = image_ref[:, pl.ds(0, band)] + halo[...]

    residual_head = res_ref[:, pl.ds(0, band)]
    image_head = image_ref[:, pl.ds(0, band)]
    along = along_rest + jnp.sum(residual_head * image_head, axis=1, keepdims=True)
    energy = energy_rest + jnp.sum(image_head * image_head, axis=1, keepdims=True)

    @pl.when(my_sub < n_sub - 1)
    def _():
        halo_copy(my_sub + 1).wait_send()

    width = rows // 3
    along = along[0:width] + along[width : 2 * width] + along[2 * width :]
    energy = energy[0:width] + energy[width : 2 * width] + energy[2 * width :]
    lane = lax.broadcasted_iota(jnp.int32, (8, 128), 1)
    block = jnp.zeros((8, 128), jnp.float32)
    for k in range(width // 8):
        block = jnp.where(lane == k, along[8 * k : 8 * k + 8], block)
        block = jnp.where(lane == width // 8 + k, energy[8 * k : 8 * k + 8], block)

    def exchange(value, first, count, my_index, device_of):
        slots[first + my_index] = value
        sends = []
        for d in range(1, count):
            copy = pltpu.make_async_remote_copy(
                src_ref=slots.at[first + my_index],
                dst_ref=slots.at[first + my_index],
                send_sem=send_sem.at[first + d],
                recv_sem=recv_sem.at[first + my_index],
                device_id=device_of((my_index + d) % count),
                device_id_type=MESH,
            )
            copy.start()
            sends.append(copy)
        for d in range(1, count):
            source = (my_index + count - d) % count
            pltpu.make_async_remote_copy(
                src_ref=slots.at[first + source],
                dst_ref=slots.at[first + source],
                send_sem=send_sem.at[first + d],
                recv_sem=recv_sem.at[first + source],
                device_id=device_of(source),
                device_id_type=MESH,
            ).wait_recv()
        for copy in sends:
            copy.wait_send()
        total = slots[first]
        for i in range(1, count):
            total = total + slots[first + i]
        return total

    partial_sum = exchange(block, 0, n_sub, my_sub, lambda i: (my_grp, i))
    sums_ref[...] = exchange(partial_sum, n_sub, n_grp, my_grp, lambda i: (i, my_sub))


def image_and_sums(residual, partial_sum, call):
    n_grp = lax.axis_size("grp")
    n_sub = lax.axis_size("sub")
    rows, own_count = residual.shape
    band = partial_sum.shape[1] - own_count
    width = rows // 3
    image, sums = pl.pallas_call(
        functools.partial(image_sums_kernel, n_grp, n_sub),
        out_shape=(
            jax.ShapeDtypeStruct((rows, own_count), jnp.float32),
            jax.ShapeDtypeStruct((8, 128), jnp.float32),
        ),
        in_specs=[pl.BlockSpec(memory_space=pltpu.VMEM)] * 2,
        out_specs=(pl.BlockSpec(memory_space=pltpu.VMEM),) * 2,
        scratch_shapes=[
            pltpu.VMEM((rows, band), jnp.float32),
            pltpu.VMEM((n_sub + n_grp, 8, 128), jnp.float32),
            pltpu.SemaphoreType.DMA((n_sub + n_grp,)),
            pltpu.SemaphoreType.DMA((n_sub + n_grp,)),
            pltpu.SemaphoreType.DMA(()),
            pltpu.SemaphoreType.DMA(()),
        ],
        compiler_params=pltpu.CompilerParams(collective_id=call, has_side_effects=True),
    )(residual, partial_sum)
    columns = width // 8
    along = sums[:, :columns].T.reshape(width)
    energy = sums[:, columns : 2 * columns].T.reshape(width)
    return image, along, energy


def column_sums(first, second):
    return jnp.sum((first * second).reshape(3, -1, first.shape[1]), axis=(0, 2))


def update(solution, residual, image, along, energy):
    alpha = along / (energy + epsilon)
    scale_rows = jnp.tile(alpha, 3)[:, None]
    return (solution + scale_rows * residual, residual - scale_rows * image)


def shards(rhs, blocks, owners, conn):
    groups = lax.axis_size("grp")
    held = blocks.shape[0]
    capacity = max(2, 3 * held // 8)
    send_blocks, send_links = place_blocks(blocks, owners, conn, groups, capacity)
    got_blocks, got_links = (
        lax.all_to_all(send_blocks, "grp", split_axis=0, concat_axis=0, tiled=True),
        lax.all_to_all(send_links, "grp", split_axis=0, concat_axis=0, tiled=True),
    )
    matrices = got_blocks[:, :, :6561].reshape(groups * capacity, 81, 81)
    residual = rhs
    solution = jnp.zeros(rhs.shape, jnp.float32)
    own_count = rhs.shape[1]
    band_width = 2 * held
    local_links = jnp.clip(
        got_links - lax.axis_index("sub") * own_count, 0, own_count + band_width - 1
    ).astype(jnp.int32)
    places = jnp.arange(own_count + band_width, dtype=jnp.int32)
    selector = (places[:, None] == local_links.reshape(1, -1)).astype(jnp.bfloat16)
    for step in range(STEPS):
        rounded = residual.astype(jnp.bfloat16)
        upper = passed_along(rounded[:, :band_width], "sub", -1)
        split = local_links.reshape(1, -1) if step else None
        partial_sum = element_products(matrices, selector, rounded, upper, split)
        image, along, energy = image_and_sums(residual, partial_sum, step)
        solution, residual = update(solution, residual, image, along, energy)
    return (solution, residual)


def solution(mesh):
    return jax.shard_map(
        shards,
        mesh=mesh,
        in_specs=(
            P(None, ("grp", "sub")),
            P(("grp", "sub"), None),
            P(("grp", "sub"), None),
            P(("grp", "sub"), None),
        ),
        out_specs=(P(None, ("grp", "sub")), P(None, ("grp", "sub"))),
        check_vma=False,
    )
```

```python
import functools

import jax
import jax.numpy as jnp
from jax import lax
from jax.experimental import pallas as pl
from jax.experimental.pallas import tpu as pltpu
from jax.sharding import PartitionSpec as P

MESH = pl.DeviceIdType.MESH

STEPS = 2


epsilon = 1e-06


def passed_along(block, axis, distance):
    devices = range(lax.axis_size(axis))
    route = [(i - distance, i) for i in devices if i - distance in devices]
    return lax.ppermute(block, axis, route)


def place_blocks(blocks, owners, conn, groups, capacity):
    owner_group = owners[:, 0]
    onehot = (owner_group[:, None] == jnp.arange(groups, dtype=jnp.int32)[None, :]).astype(
        jnp.int32
    )
    before = jnp.cumsum(onehot, axis=0) - onehot
    position = jnp.sum(before * onehot, axis=1)
    target = owner_group * capacity + position
    send_blocks = (
        jnp.zeros((groups * capacity, blocks.shape[1]), blocks.dtype).at[target].set(blocks)
    )
    send_links = jnp.zeros((groups * capacity, conn.shape[1]), jnp.int32).at[target].set(conn)
    return (send_blocks.reshape(groups, capacity, -1), send_links.reshape(groups, capacity, -1))


def element_products(matrices, selector, own_field, upper_field, split):
    rows = own_field.shape[0]
    own_count = own_field.shape[1]
    count = matrices.shape[0]
    contract = (((0,), (1,)), ((), ()))
    if split is not None:
        links = split
        own_places = jnp.arange(own_count, dtype=jnp.int32)
        upper_places = jnp.arange(upper_field.shape[1], dtype=jnp.int32) + own_count
        own_selector = (own_places[:, None] == links).astype(jnp.bfloat16)
        upper_selector = (upper_places[:, None] == links).astype(jnp.bfloat16)
        picked = lax.dot_general(
            own_selector, own_field, contract, preferred_element_type=jnp.float32
        )
        picked = picked + lax.dot_general(
            upper_selector, upper_field, contract, preferred_element_type=jnp.float32
        )
    else:
        field = jnp.concatenate([own_field, upper_field], axis=1)
        picked = lax.dot_general(selector, field, contract, preferred_element_type=jnp.float32)
    picked = picked.astype(jnp.bfloat16)
    picked = picked.reshape(count, 81, rows // 3)
    result = jnp.einsum("sab,sao->sbo", matrices, picked, preferred_element_type=jnp.float32)
    result = result.reshape(count * 27, rows)
    high_part = result.astype(jnp.bfloat16)
    low_part = (result - high_part.astype(jnp.float32)).astype(jnp.bfloat16)
    parts = jnp.concatenate([high_part, low_part], axis=1)
    acc = jnp.dot(selector, parts, preferred_element_type=jnp.float32)
    return (acc[:, :rows] + acc[:, rows:]).T


def image_sums_kernel(
    n_grp, n_sub, res_ref, part_ref, image_ref, sums_ref,
    halo, slots, send_sem, recv_sem, halo_send, halo_recv,
):
    my_grp = lax.axis_index("grp")
    my_sub = lax.axis_index("sub")
    own_count = image_ref.shape[1]
    band = halo.shape[1]
    rows = res_ref.shape[0]
    barrier = pltpu.get_barrier_semaphore()
    for d in range(1, n_sub):
        target = (my_grp, (my_sub + d) % n_sub)
        pl.semaphore_signal(barrier, inc=1, device_id=target, device_id_type=MESH)
    for d in range(1, n_grp):
        target = ((my_grp + d) % n_grp, my_sub)
        pl.semaphore_signal(barrier, inc=1, device_id=target, device_id_type=MESH)
    image_ref[...] = part_ref[:, pl.ds(0, own_count)]
    rest = own_count - band
    residual_rest = res_ref[:, pl.ds(band, rest)]
    image_rest = image_ref[:, pl.ds(band, rest)]
    along_rest = jnp.sum(residual_rest * image_rest, axis=1, keepdims=True)
    energy_rest = jnp.sum(image_rest * image_rest, axis=1, keepdims=True)
    pl.semaphore_wait(barrier, n_sub - 1 + n_grp - 1)

    def halo_copy(target_sub):
        return pltpu.make_async_remote_copy(
            src_ref=part_ref.at[:, pl.ds(own_count, band)],
            dst_ref=halo,
            send_sem=halo_send,
            recv_sem=halo_recv,
            device_id=(my_grp, target_sub),
            device_id_type=MESH,
        )

    @pl.when(my_sub < n_sub - 1)
    def _():
        halo_copy(my_sub + 1).start()

    @pl.when(my_sub > 0)
    def _():
        halo_copy(my_sub - 1).wait_recv()
        image_ref[:, pl.ds(0, band)] = image_ref[:, pl.ds(0, band)] + halo[...]

    residual_head = res_ref[:, pl.ds(0, band)]
    image_head = image_ref[:, pl.ds(0, band)]
    along = along_rest + jnp.sum(residual_head * image_head, axis=1, keepdims=True)
    energy = energy_rest + jnp.sum(image_head * image_head, axis=1, keepdims=True)

    @pl.when(my_sub < n_sub - 1)
    def _():
        halo_copy(my_sub + 1).wait_send()

    width = rows // 3
    along = along[0:width] + along[width : 2 * width] + along[2 * width :]
    energy = energy[0:width] + energy[width : 2 * width] + energy[2 * width :]
    lane = lax.broadcasted_iota(jnp.int32, (8, 128), 1)
    block = jnp.zeros((8, 128), jnp.float32)
    for k in range(width // 8):
        block = jnp.where(lane == k, along[8 * k : 8 * k + 8], block)
        block = jnp.where(lane == width // 8 + k, energy[8 * k : 8 * k + 8], block)

    def exchange(value, first, count, my_index, device_of):
        slots[first + my_index] = value
        sends = []
        for d in range(1, count):
            copy = pltpu.make_async_remote_copy(
                src_ref=slots.at[first + my_index],
                dst_ref=slots.at[first + my_index],
                send_sem=send_sem.at[first + d],
                recv_sem=recv_sem.at[first + my_index],
                device_id=device_of((my_index + d) % count),
                device_id_type=MESH,
            )
            copy.start()
            sends.append(copy)
        for d in range(1, count):
            source = (my_index + count - d) % count
            pltpu.make_async_remote_copy(
                src_ref=slots.at[first + source],
                dst_ref=slots.at[first + source],
                send_sem=send_sem.at[first + d],
                recv_sem=recv_sem.at[first + source],
                device_id=device_of(source),
                device_id_type=MESH,
            ).wait_recv()
        for copy in sends:
            copy.wait_send()
        total = slots[first]
        for i in range(1, count):
            total = total + slots[first + i]
        return total

    partial_sum = exchange(block, 0, n_grp, my_grp, lambda i: (i, my_sub))
    sums_ref[...] = exchange(partial_sum, n_grp, n_sub, my_sub, lambda i: (my_grp, i))


def image_and_sums(residual, partial_sum, call):
    n_grp = lax.axis_size("grp")
    n_sub = lax.axis_size("sub")
    rows, own_count = residual.shape
    band = partial_sum.shape[1] - own_count
    width = rows // 3
    image, sums = pl.pallas_call(
        functools.partial(image_sums_kernel, n_grp, n_sub),
        out_shape=(
            jax.ShapeDtypeStruct((rows, own_count), jnp.float32),
            jax.ShapeDtypeStruct((8, 128), jnp.float32),
        ),
        in_specs=[pl.BlockSpec(memory_space=pltpu.VMEM)] * 2,
        out_specs=(pl.BlockSpec(memory_space=pltpu.VMEM),) * 2,
        scratch_shapes=[
            pltpu.VMEM((rows, band), jnp.float32),
            pltpu.VMEM((n_sub + n_grp, 8, 128), jnp.float32),
            pltpu.SemaphoreType.DMA((n_sub + n_grp,)),
            pltpu.SemaphoreType.DMA((n_sub + n_grp,)),
            pltpu.SemaphoreType.DMA(()),
            pltpu.SemaphoreType.DMA(()),
        ],
        compiler_params=pltpu.CompilerParams(collective_id=call, has_side_effects=True),
    )(residual, partial_sum)
    columns = width // 8
    along = sums[:, :columns].T.reshape(width)
    energy = sums[:, columns : 2 * columns].T.reshape(width)
    return image, along, energy


def column_sums(first, second):
    return jnp.sum((first * second).reshape(3, -1, first.shape[1]), axis=(0, 2))


def update(solution, residual, image, along, energy):
    alpha = along / (energy + epsilon)
    scale_rows = jnp.tile(alpha, 3)[:, None]
    return (solution + scale_rows * residual, residual - scale_rows * image)


def shards(rhs, blocks, owners, conn):
    groups = lax.axis_size("grp")
    held = blocks.shape[0]
    capacity = max(2, 3 * held // 8)
    send_blocks, send_links = place_blocks(blocks, owners, conn, groups, capacity)
    got_blocks, got_links = (
        lax.all_to_all(send_blocks, "grp", split_axis=0, concat_axis=0, tiled=True),
        lax.all_to_all(send_links, "grp", split_axis=0, concat_axis=0, tiled=True),
    )
    matrices = got_blocks[:, :, :6561].reshape(groups * capacity, 81, 81)
    residual = rhs
    solution = jnp.zeros(rhs.shape, jnp.float32)
    own_count = rhs.shape[1]
    band_width = 2 * held
    local_links = jnp.clip(
        got_links - lax.axis_index("sub") * own_count, 0, own_count + band_width - 1
    ).astype(jnp.int32)
    places = jnp.arange(own_count + band_width, dtype=jnp.int32)
    selector = (places[:, None] == local_links.reshape(1, -1)).astype(jnp.bfloat16)
    for step in range(STEPS):
        rounded = residual.astype(jnp.bfloat16)
        upper = passed_along(rounded[:, :band_width], "sub", -1)
        split = local_links.reshape(1, -1) if step else None
        partial_sum = element_products(matrices, selector, rounded, upper, split)
        image, along, energy = image_and_sums(residual, partial_sum, step)
        solution, residual = update(solution, residual, image, along, energy)
    return (solution, residual)


def solution(mesh):
    return jax.shard_map(
        shards,
        mesh=mesh,
        in_specs=(
            P(None, ("grp", "sub")),
            P(("grp", "sub"), None),
            P(("grp", "sub"), None),
            P(("grp", "sub"), None),
        ),
        out_specs=(P(None, ("grp", "sub")), P(None, ("grp", "sub"))),
        check_vma=False,
    )
```

```python
import functools

import jax
import jax.numpy as jnp
from jax import lax
from jax.experimental import pallas as pl
from jax.experimental.pallas import tpu as pltpu
from jax.sharding import PartitionSpec as P

MESH = pl.DeviceIdType.MESH

STEPS = 2


epsilon = 1e-06


def passed_along(block, axis, distance):
    devices = range(lax.axis_size(axis))
    route = [(i - distance, i) for i in devices if i - distance in devices]
    return lax.ppermute(block, axis, route)


def place_blocks(blocks, owners, conn, groups, capacity):
    owner_group = owners[:, 0]
    onehot = (owner_group[:, None] == jnp.arange(groups, dtype=jnp.int32)[None, :]).astype(
        jnp.int32
    )
    before = jnp.cumsum(onehot, axis=0) - onehot
    position = jnp.sum(before * onehot, axis=1)
    target = owner_group * capacity + position
    send_blocks = (
        jnp.zeros((groups * capacity, blocks.shape[1]), blocks.dtype).at[target].set(blocks)
    )
    send_links = jnp.zeros((groups * capacity, conn.shape[1]), jnp.int32).at[target].set(conn)
    return (send_blocks.reshape(groups, capacity, -1), send_links.reshape(groups, capacity, -1))


def element_products(matrices, selector, own_field, upper_field, split):
    rows = own_field.shape[0]
    own_count = own_field.shape[1]
    count = matrices.shape[0]
    contract = (((0,), (1,)), ((), ()))
    if split is not None:
        links = split
        own_places = jnp.arange(own_count, dtype=jnp.int32)
        upper_places = jnp.arange(upper_field.shape[1], dtype=jnp.int32) + own_count
        own_selector = (own_places[:, None] == links).astype(jnp.bfloat16)
        upper_selector = (upper_places[:, None] == links).astype(jnp.bfloat16)
        picked = lax.dot_general(
            own_selector, own_field, contract, preferred_element_type=jnp.float32
        )
        picked = picked + lax.dot_general(
            upper_selector, upper_field, contract, preferred_element_type=jnp.float32
        )
    else:
        field = jnp.concatenate([own_field, upper_field], axis=1)
        picked = lax.dot_general(selector, field, contract, preferred_element_type=jnp.float32)
    picked = picked.astype(jnp.bfloat16)
    picked = picked.reshape(count, 81, rows // 3)
    result = jnp.einsum("sab,sao->sbo", matrices, picked, preferred_element_type=jnp.float32)
    result = result.reshape(count * 27, rows)
    high_part = result.astype(jnp.bfloat16)
    low_part = (result - high_part.astype(jnp.float32)).astype(jnp.bfloat16)
    parts = jnp.concatenate([high_part, low_part], axis=1)
    acc = jnp.dot(selector, parts, preferred_element_type=jnp.float32)
    return (acc[:, :rows] + acc[:, rows:]).T


def image_sums_kernel(
    n_grp, n_sub, res_ref, part_ref, image_ref, sums_ref,
    halo, slots, send_sem, recv_sem, halo_send, halo_recv,
):
    my_grp = lax.axis_index("grp")
    my_sub = lax.axis_index("sub")
    own_count = image_ref.shape[1]
    band = halo.shape[1]
    rows = res_ref.shape[0]
    barrier = pltpu.get_barrier_semaphore()
    for d in range(1, n_sub):
        target = (my_grp, (my_sub + d) % n_sub)
        pl.semaphore_signal(barrier, inc=1, device_id=target, device_id_type=MESH)
    for d in range(1, n_grp):
        target = ((my_grp + d) % n_grp, my_sub)
        pl.semaphore_signal(barrier, inc=1, device_id=target, device_id_type=MESH)
    image_ref[...] = part_ref[:, pl.ds(0, own_count)]
    rest = own_count - band
    residual_rest = res_ref[:, pl.ds(band, rest)]
    image_rest = image_ref[:, pl.ds(band, rest)]
    along_rest = jnp.sum(residual_rest * image_rest, axis=1, keepdims=True)
    energy_rest = jnp.sum(image_rest * image_rest, axis=1, keepdims=True)
    pl.semaphore_wait(barrier, n_sub - 1 + n_grp - 1)

    def halo_copy(target_sub):
        return pltpu.make_async_remote_copy(
            src_ref=part_ref.at[:, pl.ds(own_count, band)],
            dst_ref=halo,
            send_sem=halo_send,
            recv_sem=halo_recv,
            device_id=(my_grp, target_sub),
            device_id_type=MESH,
        )

    @pl.when(my_sub < n_sub - 1)
    def _():
        halo_copy(my_sub + 1).start()

    @pl.when(my_sub > 0)
    def _():
        halo_copy(my_sub - 1).wait_recv()
        image_ref[:, pl.ds(0, band)] = image_ref[:, pl.ds(0, band)] + halo[...]

    residual_head = res_ref[:, pl.ds(0, band)]
    image_head = image_ref[:, pl.ds(0, band)]
    along = along_rest + jnp.sum(residual_head * image_head, axis=1, keepdims=True)
    energy = energy_rest + jnp.sum(image_head * image_head, axis=1, keepdims=True)

    @pl.when(my_sub < n_sub - 1)
    def _():
        halo_copy(my_sub + 1).wait_send()

    width = rows // 3
    along = along[0:width] + along[width : 2 * width] + along[2 * width :]
    energy = energy[0:width] + energy[width : 2 * width] + energy[2 * width :]
    lane = lax.broadcasted_iota(jnp.int32, (8, 128), 1)
    block = jnp.zeros((8, 128), jnp.float32)
    for k in range(width // 8):
        block = jnp.where(lane == k, along[8 * k : 8 * k + 8], block)
        block = jnp.where(lane == width // 8 + k, energy[8 * k : 8 * k + 8], block)

    def exchange(value, first, count, my_index, device_of):
        slots[first + my_index] = value
        sends = []
        for d in range(1, count):
            copy = pltpu.make_async_remote_copy(
                src_ref=slots.at[first + my_index],
                dst_ref=slots.at[first + my_index],
                send_sem=send_sem.at[first + d],
                recv_sem=recv_sem.at[first + my_index],
                device_id=device_of((my_index + d) % count),
                device_id_type=MESH,
            )
            copy.start()
            sends.append(copy)
        for d in range(1, count):
            source = (my_index + count - d) % count
            pltpu.make_async_remote_copy(
                src_ref=slots.at[first + source],
                dst_ref=slots.at[first + source],
                send_sem=send_sem.at[first + d],
                recv_sem=recv_sem.at[first + source],
                device_id=device_of(source),
                device_id_type=MESH,
            ).wait_recv()
        for copy in sends:
            copy.wait_send()
        total = slots[first]
        for i in range(1, count):
            total = total + slots[first + i]
        return total

    partial_sum = exchange(block, 0, n_grp, my_grp, lambda i: (i, my_sub))
    sums_ref[...] = exchange(partial_sum, n_grp, n_sub, my_sub, lambda i: (my_grp, i))


def image_and_sums(residual, partial_sum, call):
    n_grp = lax.axis_size("grp")
    n_sub = lax.axis_size("sub")
    rows, own_count = residual.shape
    band = partial_sum.shape[1] - own_count
    width = rows // 3
    image, sums = pl.pallas_call(
        functools.partial(image_sums_kernel, n_grp, n_sub),
        out_shape=(
            jax.ShapeDtypeStruct((rows, own_count), jnp.float32),
            jax.ShapeDtypeStruct((8, 128), jnp.float32),
        ),
        in_specs=[pl.BlockSpec(memory_space=pltpu.VMEM)] * 2,
        out_specs=(pl.BlockSpec(memory_space=pltpu.VMEM),) * 2,
        scratch_shapes=[
            pltpu.VMEM((rows, band), jnp.float32),
            pltpu.VMEM((n_sub + n_grp, 8, 128), jnp.float32),
            pltpu.SemaphoreType.DMA((n_sub + n_grp,)),
            pltpu.SemaphoreType.DMA((n_sub + n_grp,)),
            pltpu.SemaphoreType.DMA(()),
            pltpu.SemaphoreType.DMA(()),
        ],
        compiler_params=pltpu.CompilerParams(collective_id=call, has_side_effects=True),
    )(residual, partial_sum)
    columns = width // 8
    along = sums[:, :columns].T.reshape(width)
    energy = sums[:, columns : 2 * columns].T.reshape(width)
    return image, along, energy


def column_sums(first, second):
    return jnp.sum((first * second).reshape(3, -1, first.shape[1]), axis=(0, 2))


def update(solution, residual, image, along, energy):
    alpha = along / (energy + epsilon)
    scale_rows = jnp.tile(alpha, 3)[:, None]
    return (solution + scale_rows * residual, residual - scale_rows * image)


def shards(rhs, blocks, owners, conn):
    groups = lax.axis_size("grp")
    held = blocks.shape[0]
    capacity = max(2, 3 * held // 8)
    send_blocks, send_links = lax.optimization_barrier(
        place_blocks(blocks, owners, conn, groups, capacity)
    )
    got_blocks, got_links = (
        lax.all_to_all(send_blocks, "grp", split_axis=0, concat_axis=0, tiled=True),
        lax.all_to_all(send_links, "grp", split_axis=0, concat_axis=0, tiled=True),
    )
    matrices = got_blocks[:, :, :6561].reshape(groups * capacity, 81, 81)
    residual = rhs
    solution = jnp.zeros(rhs.shape, jnp.float32)
    own_count = rhs.shape[1]
    band_width = 2 * held
    local_links = jnp.clip(
        got_links - lax.axis_index("sub") * own_count, 0, own_count + band_width - 1
    ).astype(jnp.int32)
    places = jnp.arange(own_count + band_width, dtype=jnp.int32)
    selector = (places[:, None] == local_links.reshape(1, -1)).astype(jnp.bfloat16)
    for step in range(STEPS):
        rounded = residual.astype(jnp.bfloat16)
        upper = passed_along(rounded[:, :band_width], "sub", -1)
        split = local_links.reshape(1, -1) if step else None
        partial_sum = element_products(matrices, selector, rounded, upper, split)
        image, along, energy = image_and_sums(residual, partial_sum, step)
        solution, residual = update(solution, residual, image, along, energy)
    return (solution, residual)


def solution(mesh):
    return jax.shard_map(
        shards,
        mesh=mesh,
        in_specs=(
            P(None, ("grp", "sub")),
            P(("grp", "sub"), None),
            P(("grp", "sub"), None),
            P(("grp", "sub"), None),
        ),
        out_specs=(P(None, ("grp", "sub")), P(None, ("grp", "sub"))),
        check_vma=False,
    )
```

```python
import functools

import jax
import jax.numpy as jnp
from jax import lax
from jax.experimental import pallas as pl
from jax.experimental.pallas import tpu as pltpu
from jax.sharding import PartitionSpec as P

MESH = pl.DeviceIdType.MESH

STEPS = 2


epsilon = 1e-06


def passed_along(block, axis, distance):
    devices = range(lax.axis_size(axis))
    route = [(i - distance, i) for i in devices if i - distance in devices]
    return lax.ppermute(block, axis, route)


def place_blocks(blocks, owners, conn, groups, capacity):
    owner_group = owners[:, 0]
    onehot = (owner_group[:, None] == jnp.arange(groups, dtype=jnp.int32)[None, :]).astype(
        jnp.int32
    )
    rows = jnp.arange(owner_group.shape[0], dtype=jnp.int32)
    earlier = (rows[:, None] > rows[None, :]).astype(jnp.bfloat16)
    before = jnp.dot(earlier, onehot.astype(jnp.bfloat16), preferred_element_type=jnp.float32)
    position = jnp.sum(before.astype(jnp.int32) * onehot, axis=1)
    target = owner_group * capacity + position
    send_blocks = (
        jnp.zeros((groups * capacity, blocks.shape[1]), blocks.dtype).at[target].set(blocks)
    )
    send_links = jnp.zeros((groups * capacity, conn.shape[1]), jnp.int32).at[target].set(conn)
    return (send_blocks.reshape(groups, capacity, -1), send_links.reshape(groups, capacity, -1))


def element_products(matrices, selector, own_field, upper_field, split):
    rows = own_field.shape[0]
    own_count = own_field.shape[1]
    count = matrices.shape[0]
    contract = (((0,), (1,)), ((), ()))
    if split is not None:
        links = split
        own_places = jnp.arange(own_count, dtype=jnp.int32)
        upper_places = jnp.arange(upper_field.shape[1], dtype=jnp.int32) + own_count
        own_selector = (own_places[:, None] == links).astype(jnp.bfloat16)
        upper_selector = (upper_places[:, None] == links).astype(jnp.bfloat16)
        picked = lax.dot_general(
            own_selector, own_field, contract, preferred_element_type=jnp.float32
        )
        picked = picked + lax.dot_general(
            upper_selector, upper_field, contract, preferred_element_type=jnp.float32
        )
    else:
        field = jnp.concatenate([own_field, upper_field], axis=1)
        picked = lax.dot_general(selector, field, contract, preferred_element_type=jnp.float32)
    picked = picked.astype(jnp.bfloat16)
    picked = picked.reshape(count, 81, rows // 3)
    result = jnp.einsum("sab,sao->sbo", matrices, picked, preferred_element_type=jnp.float32)
    result = result.reshape(count * 27, rows)
    high_part = result.astype(jnp.bfloat16)
    low_part = (result - high_part.astype(jnp.float32)).astype(jnp.bfloat16)
    parts = jnp.concatenate([high_part, low_part], axis=1)
    acc = jnp.dot(selector, parts, preferred_element_type=jnp.float32)
    return (acc[:, :rows] + acc[:, rows:]).T


def image_sums_kernel(
    n_grp, n_sub, res_ref, part_ref, image_ref, sums_ref,
    halo, slots, send_sem, recv_sem, halo_send, halo_recv,
):
    my_grp = lax.axis_index("grp")
    my_sub = lax.axis_index("sub")
    own_count = image_ref.shape[1]
    band = halo.shape[1]
    rows = res_ref.shape[0]
    barrier = pltpu.get_barrier_semaphore()
    for d in range(1, n_sub):
        target = (my_grp, (my_sub + d) % n_sub)
        pl.semaphore_signal(barrier, inc=1, device_id=target, device_id_type=MESH)
    for d in range(1, n_grp):
        target = ((my_grp + d) % n_grp, my_sub)
        pl.semaphore_signal(barrier, inc=1, device_id=target, device_id_type=MESH)
    image_ref[...] = part_ref[:, pl.ds(0, own_count)]
    rest = own_count - band
    residual_rest = res_ref[:, pl.ds(band, rest)]
    image_rest = image_ref[:, pl.ds(band, rest)]
    along_rest = jnp.sum(residual_rest * image_rest, axis=1, keepdims=True)
    energy_rest = jnp.sum(image_rest * image_rest, axis=1, keepdims=True)
    pl.semaphore_wait(barrier, n_sub - 1 + n_grp - 1)

    def halo_copy(target_sub):
        return pltpu.make_async_remote_copy(
            src_ref=part_ref.at[:, pl.ds(own_count, band)],
            dst_ref=halo,
            send_sem=halo_send,
            recv_sem=halo_recv,
            device_id=(my_grp, target_sub),
            device_id_type=MESH,
        )

    @pl.when(my_sub < n_sub - 1)
    def _():
        halo_copy(my_sub + 1).start()

    @pl.when(my_sub > 0)
    def _():
        halo_copy(my_sub - 1).wait_recv()
        image_ref[:, pl.ds(0, band)] = image_ref[:, pl.ds(0, band)] + halo[...]

    residual_head = res_ref[:, pl.ds(0, band)]
    image_head = image_ref[:, pl.ds(0, band)]
    along = along_rest + jnp.sum(residual_head * image_head, axis=1, keepdims=True)
    energy = energy_rest + jnp.sum(image_head * image_head, axis=1, keepdims=True)

    @pl.when(my_sub < n_sub - 1)
    def _():
        halo_copy(my_sub + 1).wait_send()

    width = rows // 3
    along = along[0:width] + along[width : 2 * width] + along[2 * width :]
    energy = energy[0:width] + energy[width : 2 * width] + energy[2 * width :]
    lane = lax.broadcasted_iota(jnp.int32, (8, 128), 1)
    block = jnp.zeros((8, 128), jnp.float32)
    for k in range(width // 8):
        block = jnp.where(lane == k, along[8 * k : 8 * k + 8], block)
        block = jnp.where(lane == width // 8 + k, energy[8 * k : 8 * k + 8], block)

    def exchange(value, first, count, my_index, device_of):
        slots[first + my_index] = value
        sends = []
        for d in range(1, count):
            copy = pltpu.make_async_remote_copy(
                src_ref=slots.at[first + my_index],
                dst_ref=slots.at[first + my_index],
                send_sem=send_sem.at[first + d],
                recv_sem=recv_sem.at[first + my_index],
                device_id=device_of((my_index + d) % count),
                device_id_type=MESH,
            )
            copy.start()
            sends.append(copy)
        for d in range(1, count):
            source = (my_index + count - d) % count
            pltpu.make_async_remote_copy(
                src_ref=slots.at[first + source],
                dst_ref=slots.at[first + source],
                send_sem=send_sem.at[first + d],
                recv_sem=recv_sem.at[first + source],
                device_id=device_of(source),
                device_id_type=MESH,
            ).wait_recv()
        for copy in sends:
            copy.wait_send()
        total = slots[first]
        for i in range(1, count):
            total = total + slots[first + i]
        return total

    partial_sum = exchange(block, 0, n_grp, my_grp, lambda i: (i, my_sub))
    sums_ref[...] = exchange(partial_sum, n_grp, n_sub, my_sub, lambda i: (my_grp, i))


def image_and_sums(residual, partial_sum, call):
    n_grp = lax.axis_size("grp")
    n_sub = lax.axis_size("sub")
    rows, own_count = residual.shape
    band = partial_sum.shape[1] - own_count
    width = rows // 3
    image, sums = pl.pallas_call(
        functools.partial(image_sums_kernel, n_grp, n_sub),
        out_shape=(
            jax.ShapeDtypeStruct((rows, own_count), jnp.float32),
            jax.ShapeDtypeStruct((8, 128), jnp.float32),
        ),
        in_specs=[pl.BlockSpec(memory_space=pltpu.VMEM)] * 2,
        out_specs=(pl.BlockSpec(memory_space=pltpu.VMEM),) * 2,
        scratch_shapes=[
            pltpu.VMEM((rows, band), jnp.float32),
            pltpu.VMEM((n_sub + n_grp, 8, 128), jnp.float32),
            pltpu.SemaphoreType.DMA((n_sub + n_grp,)),
            pltpu.SemaphoreType.DMA((n_sub + n_grp,)),
            pltpu.SemaphoreType.DMA(()),
            pltpu.SemaphoreType.DMA(()),
        ],
        compiler_params=pltpu.CompilerParams(collective_id=call, has_side_effects=True),
    )(residual, partial_sum)
    columns = width // 8
    along = sums[:, :columns].T.reshape(width)
    energy = sums[:, columns : 2 * columns].T.reshape(width)
    return image, along, energy


def column_sums(first, second):
    return jnp.sum((first * second).reshape(3, -1, first.shape[1]), axis=(0, 2))


def update(solution, residual, image, along, energy):
    alpha = along / (energy + epsilon)
    scale_rows = jnp.tile(alpha, 3)[:, None]
    return (solution + scale_rows * residual, residual - scale_rows * image)


def shards(rhs, blocks, owners, conn):
    groups = lax.axis_size("grp")
    held = blocks.shape[0]
    capacity = max(2, 3 * held // 8)
    send_blocks, send_links = place_blocks(blocks, owners, conn, groups, capacity)
    got_blocks, got_links = (
        lax.all_to_all(send_blocks, "grp", split_axis=0, concat_axis=0, tiled=True),
        lax.all_to_all(send_links, "grp", split_axis=0, concat_axis=0, tiled=True),
    )
    matrices = got_blocks[:, :, :6561].reshape(groups * capacity, 81, 81)
    residual = rhs
    solution = jnp.zeros(rhs.shape, jnp.float32)
    own_count = rhs.shape[1]
    band_width = 2 * held
    local_links = jnp.clip(
        got_links - lax.axis_index("sub") * own_count, 0, own_count + band_width - 1
    ).astype(jnp.int32)
    places = jnp.arange(own_count + band_width, dtype=jnp.int32)
    selector = (places[:, None] == local_links.reshape(1, -1)).astype(jnp.bfloat16)
    for step in range(STEPS):
        rounded = residual.astype(jnp.bfloat16)
        upper = passed_along(rounded[:, :band_width], "sub", -1)
        split = local_links.reshape(1, -1) if step else None
        partial_sum = element_products(matrices, selector, rounded, upper, split)
        image, along, energy = image_and_sums(residual, partial_sum, step)
        solution, residual = update(solution, residual, image, along, energy)
    return (solution, residual)


def solution(mesh):
    return jax.shard_map(
        shards,
        mesh=mesh,
        in_specs=(
            P(None, ("grp", "sub")),
            P(("grp", "sub"), None),
            P(("grp", "sub"), None),
            P(("grp", "sub"), None),
        ),
        out_specs=(P(None, ("grp", "sub")), P(None, ("grp", "sub"))),
        check_vma=False,
    )
```

```python
import functools

import jax
import jax.numpy as jnp
from jax import lax
from jax.experimental import pallas as pl
from jax.experimental.pallas import tpu as pltpu
from jax.sharding import PartitionSpec as P

MESH = pl.DeviceIdType.MESH

STEPS = 2


epsilon = 1e-06


def passed_along(block, axis, distance):
    devices = range(lax.axis_size(axis))
    route = [(i - distance, i) for i in devices if i - distance in devices]
    return lax.ppermute(block, axis, route)


def place_blocks(blocks, owners, conn, groups, capacity):
    owner_group = owners[:, 0]
    onehot = (owner_group[:, None] == jnp.arange(groups, dtype=jnp.int32)[None, :]).astype(
        jnp.int32
    )
    rows = jnp.arange(owner_group.shape[0], dtype=jnp.int32)
    earlier = (rows[:, None] > rows[None, :]).astype(jnp.bfloat16)
    before = jnp.dot(earlier, onehot.astype(jnp.bfloat16), preferred_element_type=jnp.float32)
    position = jnp.sum(before.astype(jnp.int32) * onehot, axis=1)
    target = owner_group * capacity + position
    slots = jnp.arange(groups * capacity, dtype=jnp.int32)
    placement = (slots[:, None] == target[None, :]).astype(blocks.dtype)
    send_blocks = jnp.dot(placement, blocks, preferred_element_type=jnp.float32).astype(
        blocks.dtype
    )
    send_links = jnp.zeros((groups * capacity, conn.shape[1]), jnp.int32).at[target].set(conn)
    return (send_blocks.reshape(groups, capacity, -1), send_links.reshape(groups, capacity, -1))


def element_products(matrices, selector, own_field, upper_field, split):
    rows = own_field.shape[0]
    own_count = own_field.shape[1]
    count = matrices.shape[0]
    contract = (((0,), (1,)), ((), ()))
    if split is not None:
        links = split
        own_places = jnp.arange(own_count, dtype=jnp.int32)
        upper_places = jnp.arange(upper_field.shape[1], dtype=jnp.int32) + own_count
        own_selector = (own_places[:, None] == links).astype(jnp.bfloat16)
        upper_selector = (upper_places[:, None] == links).astype(jnp.bfloat16)
        picked = lax.dot_general(
            own_selector, own_field, contract, preferred_element_type=jnp.float32
        )
        picked = picked + lax.dot_general(
            upper_selector, upper_field, contract, preferred_element_type=jnp.float32
        )
    else:
        field = jnp.concatenate([own_field, upper_field], axis=1)
        picked = lax.dot_general(selector, field, contract, preferred_element_type=jnp.float32)
    picked = picked.astype(jnp.bfloat16)
    picked = picked.reshape(count, 81, rows // 3)
    result = jnp.einsum("sab,sao->sbo", matrices, picked, preferred_element_type=jnp.float32)
    result = result.reshape(count * 27, rows)
    high_part = result.astype(jnp.bfloat16)
    low_part = (result - high_part.astype(jnp.float32)).astype(jnp.bfloat16)
    parts = jnp.concatenate([high_part, low_part], axis=1)
    acc = jnp.dot(selector, parts, preferred_element_type=jnp.float32)
    return (acc[:, :rows] + acc[:, rows:]).T


def image_sums_kernel(
    n_grp, n_sub, res_ref, part_ref, image_ref, sums_ref,
    halo, slots, send_sem, recv_sem, halo_send, halo_recv,
):
    my_grp = lax.axis_index("grp")
    my_sub = lax.axis_index("sub")
    own_count = image_ref.shape[1]
    band = halo.shape[1]
    rows = res_ref.shape[0]
    barrier = pltpu.get_barrier_semaphore()
    for d in range(1, n_sub):
        target = (my_grp, (my_sub + d) % n_sub)
        pl.semaphore_signal(barrier, inc=1, device_id=target, device_id_type=MESH)
    for d in range(1, n_grp):
        target = ((my_grp + d) % n_grp, my_sub)
        pl.semaphore_signal(barrier, inc=1, device_id=target, device_id_type=MESH)
    image_ref[...] = part_ref[:, pl.ds(0, own_count)]
    rest = own_count - band
    residual_rest = res_ref[:, pl.ds(band, rest)]
    image_rest = image_ref[:, pl.ds(band, rest)]
    along_rest = jnp.sum(residual_rest * image_rest, axis=1, keepdims=True)
    energy_rest = jnp.sum(image_rest * image_rest, axis=1, keepdims=True)
    pl.semaphore_wait(barrier, n_sub - 1 + n_grp - 1)

    def halo_copy(target_sub):
        return pltpu.make_async_remote_copy(
            src_ref=part_ref.at[:, pl.ds(own_count, band)],
            dst_ref=halo,
            send_sem=halo_send,
            recv_sem=halo_recv,
            device_id=(my_grp, target_sub),
            device_id_type=MESH,
        )

    @pl.when(my_sub < n_sub - 1)
    def _():
        halo_copy(my_sub + 1).start()

    @pl.when(my_sub > 0)
    def _():
        halo_copy(my_sub - 1).wait_recv()
        image_ref[:, pl.ds(0, band)] = image_ref[:, pl.ds(0, band)] + halo[...]

    residual_head = res_ref[:, pl.ds(0, band)]
    image_head = image_ref[:, pl.ds(0, band)]
    along = along_rest + jnp.sum(residual_head * image_head, axis=1, keepdims=True)
    energy = energy_rest + jnp.sum(image_head * image_head, axis=1, keepdims=True)

    @pl.when(my_sub < n_sub - 1)
    def _():
        halo_copy(my_sub + 1).wait_send()

    width = rows // 3
    along = along[0:width] + along[width : 2 * width] + along[2 * width :]
    energy = energy[0:width] + energy[width : 2 * width] + energy[2 * width :]
    lane = lax.broadcasted_iota(jnp.int32, (8, 128), 1)
    block = jnp.zeros((8, 128), jnp.float32)
    for k in range(width // 8):
        block = jnp.where(lane == k, along[8 * k : 8 * k + 8], block)
        block = jnp.where(lane == width // 8 + k, energy[8 * k : 8 * k + 8], block)

    def exchange(value, first, count, my_index, device_of):
        slots[first + my_index] = value
        sends = []
        for d in range(1, count):
            copy = pltpu.make_async_remote_copy(
                src_ref=slots.at[first + my_index],
                dst_ref=slots.at[first + my_index],
                send_sem=send_sem.at[first + d],
                recv_sem=recv_sem.at[first + my_index],
                device_id=device_of((my_index + d) % count),
                device_id_type=MESH,
            )
            copy.start()
            sends.append(copy)
        for d in range(1, count):
            source = (my_index + count - d) % count
            pltpu.make_async_remote_copy(
                src_ref=slots.at[first + source],
                dst_ref=slots.at[first + source],
                send_sem=send_sem.at[first + d],
                recv_sem=recv_sem.at[first + source],
                device_id=device_of(source),
                device_id_type=MESH,
            ).wait_recv()
        for copy in sends:
            copy.wait_send()
        total = slots[first]
        for i in range(1, count):
            total = total + slots[first + i]
        return total

    partial_sum = exchange(block, 0, n_grp, my_grp, lambda i: (i, my_sub))
    sums_ref[...] = exchange(partial_sum, n_grp, n_sub, my_sub, lambda i: (my_grp, i))


def image_and_sums(residual, partial_sum, call):
    n_grp = lax.axis_size("grp")
    n_sub = lax.axis_size("sub")
    rows, own_count = residual.shape
    band = partial_sum.shape[1] - own_count
    width = rows // 3
    image, sums = pl.pallas_call(
        functools.partial(image_sums_kernel, n_grp, n_sub),
        out_shape=(
            jax.ShapeDtypeStruct((rows, own_count), jnp.float32),
            jax.ShapeDtypeStruct((8, 128), jnp.float32),
        ),
        in_specs=[pl.BlockSpec(memory_space=pltpu.VMEM)] * 2,
        out_specs=(pl.BlockSpec(memory_space=pltpu.VMEM),) * 2,
        scratch_shapes=[
            pltpu.VMEM((rows, band), jnp.float32),
            pltpu.VMEM((n_sub + n_grp, 8, 128), jnp.float32),
            pltpu.SemaphoreType.DMA((n_sub + n_grp,)),
            pltpu.SemaphoreType.DMA((n_sub + n_grp,)),
            pltpu.SemaphoreType.DMA(()),
            pltpu.SemaphoreType.DMA(()),
        ],
        compiler_params=pltpu.CompilerParams(collective_id=call, has_side_effects=True),
    )(residual, partial_sum)
    columns = width // 8
    along = sums[:, :columns].T.reshape(width)
    energy = sums[:, columns : 2 * columns].T.reshape(width)
    return image, along, energy


def column_sums(first, second):
    return jnp.sum((first * second).reshape(3, -1, first.shape[1]), axis=(0, 2))


def update(solution, residual, image, along, energy):
    alpha = along / (energy + epsilon)
    scale_rows = jnp.tile(alpha, 3)[:, None]
    return (solution + scale_rows * residual, residual - scale_rows * image)


def shards(rhs, blocks, owners, conn):
    groups = lax.axis_size("grp")
    held = blocks.shape[0]
    capacity = max(2, 3 * held // 8)
    send_blocks, send_links = place_blocks(blocks, owners, conn, groups, capacity)
    got_blocks, got_links = (
        lax.all_to_all(send_blocks, "grp", split_axis=0, concat_axis=0, tiled=True),
        lax.all_to_all(send_links, "grp", split_axis=0, concat_axis=0, tiled=True),
    )
    matrices = got_blocks[:, :, :6561].reshape(groups * capacity, 81, 81)
    residual = rhs
    solution = jnp.zeros(rhs.shape, jnp.float32)
    own_count = rhs.shape[1]
    band_width = 2 * held
    local_links = jnp.clip(
        got_links - lax.axis_index("sub") * own_count, 0, own_count + band_width - 1
    ).astype(jnp.int32)
    places = jnp.arange(own_count + band_width, dtype=jnp.int32)
    selector = (places[:, None] == local_links.reshape(1, -1)).astype(jnp.bfloat16)
    for step in range(STEPS):
        rounded = residual.astype(jnp.bfloat16)
        upper = passed_along(rounded[:, :band_width], "sub", -1)
        split = local_links.reshape(1, -1) if step else None
        partial_sum = element_products(matrices, selector, rounded, upper, split)
        image, along, energy = image_and_sums(residual, partial_sum, step)
        solution, residual = update(solution, residual, image, along, energy)
    return (solution, residual)


def solution(mesh):
    return jax.shard_map(
        shards,
        mesh=mesh,
        in_specs=(
            P(None, ("grp", "sub")),
            P(("grp", "sub"), None),
            P(("grp", "sub"), None),
            P(("grp", "sub"), None),
        ),
        out_specs=(P(None, ("grp", "sub")), P(None, ("grp", "sub"))),
        check_vma=False,
    )
```

```python
import functools

import jax
import jax.numpy as jnp
from jax import lax
from jax.experimental import pallas as pl
from jax.experimental.pallas import tpu as pltpu
from jax.sharding import PartitionSpec as P

MESH = pl.DeviceIdType.MESH

STEPS = 2


epsilon = 1e-06


def passed_along(block, axis, distance):
    devices = range(lax.axis_size(axis))
    route = [(i - distance, i) for i in devices if i - distance in devices]
    return lax.ppermute(block, axis, route)


def place_blocks(blocks, owners, conn, groups, capacity):
    owner_group = owners[:, 0]
    onehot = (owner_group[:, None] == jnp.arange(groups, dtype=jnp.int32)[None, :]).astype(
        jnp.int32
    )
    rows = jnp.arange(owner_group.shape[0], dtype=jnp.int32)
    earlier = (rows[:, None] > rows[None, :]).astype(jnp.bfloat16)
    before = jnp.dot(earlier, onehot.astype(jnp.bfloat16), preferred_element_type=jnp.float32)
    position = jnp.sum(before.astype(jnp.int32) * onehot, axis=1)
    target = owner_group * capacity + position
    send_blocks = (
        jnp.zeros((groups * capacity, blocks.shape[1]), blocks.dtype).at[target].set(blocks)
    )
    send_links = jnp.zeros((groups * capacity, conn.shape[1]), jnp.int32).at[target].set(conn)
    return (send_blocks.reshape(groups, capacity, -1), send_links.reshape(groups, capacity, -1))


def element_products(matrices, selector, own_field, upper_field, split):
    rows = own_field.shape[0]
    own_count = own_field.shape[1]
    count = matrices.shape[0]
    contract = (((0,), (1,)), ((), ()))
    if split is not None:
        links = split
        own_places = jnp.arange(own_count, dtype=jnp.int32)
        upper_places = jnp.arange(upper_field.shape[1], dtype=jnp.int32) + own_count
        own_selector = (own_places[:, None] == links).astype(jnp.bfloat16)
        upper_selector = (upper_places[:, None] == links).astype(jnp.bfloat16)
        picked = lax.dot_general(
            own_selector, own_field, contract, preferred_element_type=jnp.float32
        )
        picked = picked + lax.dot_general(
            upper_selector, upper_field, contract, preferred_element_type=jnp.float32
        )
    else:
        field = jnp.concatenate([own_field, upper_field], axis=1)
        picked = lax.dot_general(selector, field, contract, preferred_element_type=jnp.float32)
    picked = picked.astype(jnp.bfloat16)
    picked = picked.reshape(count, 81, rows // 3)
    result = jnp.einsum("sab,sao->sbo", matrices, picked, preferred_element_type=jnp.float32)
    result = result.reshape(count * 27, rows)
    high_part = result.astype(jnp.bfloat16)
    low_part = (result - high_part.astype(jnp.float32)).astype(jnp.bfloat16)
    parts = jnp.concatenate([high_part, low_part], axis=1)
    acc = jnp.dot(selector, parts, preferred_element_type=jnp.float32)
    return (acc[:, :rows] + acc[:, rows:]).T


def image_sums_kernel(
    n_grp, n_sub, res_ref, part_ref, image_ref, sums_ref,
    halo, slots, send_sem, recv_sem, halo_send, halo_recv,
):
    my_grp = lax.axis_index("grp")
    my_sub = lax.axis_index("sub")
    own_count = image_ref.shape[1]
    band = halo.shape[1]
    rows = res_ref.shape[0]
    barrier = pltpu.get_barrier_semaphore()
    for d in range(1, n_sub):
        target = (my_grp, (my_sub + d) % n_sub)
        pl.semaphore_signal(barrier, inc=1, device_id=target, device_id_type=MESH)
    for d in range(1, n_grp):
        target = ((my_grp + d) % n_grp, my_sub)
        pl.semaphore_signal(barrier, inc=1, device_id=target, device_id_type=MESH)
    image_ref[...] = part_ref[:, pl.ds(0, own_count)]
    rest = own_count - band
    residual_rest = res_ref[:, pl.ds(band, rest)]
    image_rest = image_ref[:, pl.ds(band, rest)]
    along_rest = jnp.sum(residual_rest * image_rest, axis=1, keepdims=True)
    energy_rest = jnp.sum(image_rest * image_rest, axis=1, keepdims=True)
    pl.semaphore_wait(barrier, n_sub - 1 + n_grp - 1)

    def halo_copy(target_sub):
        return pltpu.make_async_remote_copy(
            src_ref=part_ref.at[:, pl.ds(own_count, band)],
            dst_ref=halo,
            send_sem=halo_send,
            recv_sem=halo_recv,
            device_id=(my_grp, target_sub),
            device_id_type=MESH,
        )

    @pl.when(my_sub < n_sub - 1)
    def _():
        halo_copy(my_sub + 1).start()

    @pl.when(my_sub > 0)
    def _():
        halo_copy(my_sub - 1).wait_recv()
        image_ref[:, pl.ds(0, band)] = image_ref[:, pl.ds(0, band)] + halo[...]

    residual_head = res_ref[:, pl.ds(0, band)]
    image_head = image_ref[:, pl.ds(0, band)]
    along = along_rest + jnp.sum(residual_head * image_head, axis=1, keepdims=True)
    energy = energy_rest + jnp.sum(image_head * image_head, axis=1, keepdims=True)

    width = rows // 3
    along = along[0:width] + along[width : 2 * width] + along[2 * width :]
    energy = energy[0:width] + energy[width : 2 * width] + energy[2 * width :]
    lane = lax.broadcasted_iota(jnp.int32, (8, 128), 1)
    block = jnp.zeros((8, 128), jnp.float32)
    for k in range(width // 8):
        block = jnp.where(lane == k, along[8 * k : 8 * k + 8], block)
        block = jnp.where(lane == width // 8 + k, energy[8 * k : 8 * k + 8], block)

    def exchange(value, first, count, my_index, device_of):
        slots[first + my_index] = value
        sends = []
        for d in range(1, count):
            copy = pltpu.make_async_remote_copy(
                src_ref=slots.at[first + my_index],
                dst_ref=slots.at[first + my_index],
                send_sem=send_sem.at[first + d],
                recv_sem=recv_sem.at[first + my_index],
                device_id=device_of((my_index + d) % count),
                device_id_type=MESH,
            )
            copy.start()
            sends.append(copy)
        for d in range(1, count):
            source = (my_index + count - d) % count
            pltpu.make_async_remote_copy(
                src_ref=slots.at[first + source],
                dst_ref=slots.at[first + source],
                send_sem=send_sem.at[first + d],
                recv_sem=recv_sem.at[first + source],
                device_id=device_of(source),
                device_id_type=MESH,
            ).wait_recv()
        for copy in sends:
            copy.wait_send()
        total = slots[first]
        for i in range(1, count):
            total = total + slots[first + i]
        return total

    partial_sum = exchange(block, 0, n_grp, my_grp, lambda i: (i, my_sub))
    sums_ref[...] = exchange(partial_sum, n_grp, n_sub, my_sub, lambda i: (my_grp, i))

    @pl.when(my_sub < n_sub - 1)
    def _():
        halo_copy(my_sub + 1).wait_send()


def image_and_sums(residual, partial_sum, call):
    n_grp = lax.axis_size("grp")
    n_sub = lax.axis_size("sub")
    rows, own_count = residual.shape
    band = partial_sum.shape[1] - own_count
    width = rows // 3
    image, sums = pl.pallas_call(
        functools.partial(image_sums_kernel, n_grp, n_sub),
        out_shape=(
            jax.ShapeDtypeStruct((rows, own_count), jnp.float32),
            jax.ShapeDtypeStruct((8, 128), jnp.float32),
        ),
        in_specs=[pl.BlockSpec(memory_space=pltpu.VMEM)] * 2,
        out_specs=(pl.BlockSpec(memory_space=pltpu.VMEM),) * 2,
        scratch_shapes=[
            pltpu.VMEM((rows, band), jnp.float32),
            pltpu.VMEM((n_sub + n_grp, 8, 128), jnp.float32),
            pltpu.SemaphoreType.DMA((n_sub + n_grp,)),
            pltpu.SemaphoreType.DMA((n_sub + n_grp,)),
            pltpu.SemaphoreType.DMA(()),
            pltpu.SemaphoreType.DMA(()),
        ],
        compiler_params=pltpu.CompilerParams(collective_id=call, has_side_effects=True),
    )(residual, partial_sum)
    columns = width // 8
    along = sums[:, :columns].T.reshape(width)
    energy = sums[:, columns : 2 * columns].T.reshape(width)
    return image, along, energy


def column_sums(first, second):
    return jnp.sum((first * second).reshape(3, -1, first.shape[1]), axis=(0, 2))


def update(solution, residual, image, along, energy):
    alpha = along / (energy + epsilon)
    scale_rows = jnp.tile(alpha, 3)[:, None]
    return (solution + scale_rows * residual, residual - scale_rows * image)


def shards(rhs, blocks, owners, conn):
    groups = lax.axis_size("grp")
    held = blocks.shape[0]
    capacity = max(2, 3 * held // 8)
    send_blocks, send_links = place_blocks(blocks, owners, conn, groups, capacity)
    got_blocks, got_links = (
        lax.all_to_all(send_blocks, "grp", split_axis=0, concat_axis=0, tiled=True),
        lax.all_to_all(send_links, "grp", split_axis=0, concat_axis=0, tiled=True),
    )
    matrices = got_blocks[:, :, :6561].reshape(groups * capacity, 81, 81)
    residual = rhs
    solution = jnp.zeros(rhs.shape, jnp.float32)
    own_count = rhs.shape[1]
    band_width = 2 * held
    local_links = jnp.clip(
        got_links - lax.axis_index("sub") * own_count, 0, own_count + band_width - 1
    ).astype(jnp.int32)
    places = jnp.arange(own_count + band_width, dtype=jnp.int32)
    selector = (places[:, None] == local_links.reshape(1, -1)).astype(jnp.bfloat16)
    for step in range(STEPS):
        rounded = residual.astype(jnp.bfloat16)
        upper = passed_along(rounded[:, :band_width], "sub", -1)
        split = local_links.reshape(1, -1) if step else None
        partial_sum = element_products(matrices, selector, rounded, upper, split)
        image, along, energy = image_and_sums(residual, partial_sum, step)
        solution, residual = update(solution, residual, image, along, energy)
    return (solution, residual)


def solution(mesh):
    return jax.shard_map(
        shards,
        mesh=mesh,
        in_specs=(
            P(None, ("grp", "sub")),
            P(("grp", "sub"), None),
            P(("grp", "sub"), None),
            P(("grp", "sub"), None),
        ),
        out_specs=(P(None, ("grp", "sub")), P(None, ("grp", "sub"))),
        check_vma=False,
    )
```

```python
import functools

import jax
import jax.numpy as jnp
from jax import lax
from jax.experimental import pallas as pl
from jax.experimental.pallas import tpu as pltpu
from jax.sharding import PartitionSpec as P

MESH = pl.DeviceIdType.MESH

STEPS = 2


epsilon = 1e-06


def passed_along(block, axis, distance):
    devices = range(lax.axis_size(axis))
    route = [(i - distance, i) for i in devices if i - distance in devices]
    return lax.ppermute(block, axis, route)


def place_blocks(blocks, owners, conn, groups, capacity):
    owner_group = owners[:, 0]
    onehot = (owner_group[:, None] == jnp.arange(groups, dtype=jnp.int32)[None, :]).astype(
        jnp.int32
    )
    rows = jnp.arange(owner_group.shape[0], dtype=jnp.int32)
    earlier = (rows[:, None] > rows[None, :]).astype(jnp.bfloat16)
    before = jnp.dot(earlier, onehot.astype(jnp.bfloat16), preferred_element_type=jnp.float32)
    position = jnp.sum(before.astype(jnp.int32) * onehot, axis=1)
    target = owner_group * capacity + position
    send_blocks = (
        jnp.zeros((groups * capacity, blocks.shape[1]), blocks.dtype).at[target].set(blocks)
    )
    send_links = jnp.zeros((groups * capacity, conn.shape[1]), jnp.int32).at[target].set(conn)
    return (send_blocks.reshape(groups, capacity, -1), send_links.reshape(groups, -1))


def element_products(matrices, selector, own_field, upper_field, split):
    rows = own_field.shape[0]
    own_count = own_field.shape[1]
    count = matrices.shape[0]
    contract = (((0,), (1,)), ((), ()))
    if split is not None:
        links = split
        own_places = jnp.arange(own_count, dtype=jnp.int32)
        upper_places = jnp.arange(upper_field.shape[1], dtype=jnp.int32) + own_count
        own_selector = (own_places[:, None] == links).astype(jnp.bfloat16)
        upper_selector = (upper_places[:, None] == links).astype(jnp.bfloat16)
        picked = lax.dot_general(
            own_selector, own_field, contract, preferred_element_type=jnp.float32
        )
        picked = picked + lax.dot_general(
            upper_selector, upper_field, contract, preferred_element_type=jnp.float32
        )
    else:
        field = jnp.concatenate([own_field, upper_field], axis=1)
        picked = lax.dot_general(selector, field, contract, preferred_element_type=jnp.float32)
    picked = picked.astype(jnp.bfloat16)
    picked = picked.reshape(count, 81, rows // 3)
    result = jnp.einsum("sab,sao->sbo", matrices, picked, preferred_element_type=jnp.float32)
    result = result.reshape(count * 27, rows)
    high_part = result.astype(jnp.bfloat16)
    low_part = (result - high_part.astype(jnp.float32)).astype(jnp.bfloat16)
    parts = jnp.concatenate([high_part, low_part], axis=1)
    acc = jnp.dot(selector, parts, preferred_element_type=jnp.float32)
    return (acc[:, :rows] + acc[:, rows:]).T


def image_sums_kernel(
    n_grp, n_sub, res_ref, part_ref, image_ref, sums_ref,
    halo, slots, send_sem, recv_sem, halo_send, halo_recv,
):
    my_grp = lax.axis_index("grp")
    my_sub = lax.axis_index("sub")
    own_count = image_ref.shape[1]
    band = halo.shape[1]
    rows = res_ref.shape[0]
    barrier = pltpu.get_barrier_semaphore()
    for d in range(1, n_sub):
        target = (my_grp, (my_sub + d) % n_sub)
        pl.semaphore_signal(barrier, inc=1, device_id=target, device_id_type=MESH)
    for d in range(1, n_grp):
        target = ((my_grp + d) % n_grp, my_sub)
        pl.semaphore_signal(barrier, inc=1, device_id=target, device_id_type=MESH)
    image_ref[...] = part_ref[:, pl.ds(0, own_count)]
    rest = own_count - band
    residual_rest = res_ref[:, pl.ds(band, rest)]
    image_rest = image_ref[:, pl.ds(band, rest)]
    along_rest = jnp.sum(residual_rest * image_rest, axis=1, keepdims=True)
    energy_rest = jnp.sum(image_rest * image_rest, axis=1, keepdims=True)
    pl.semaphore_wait(barrier, n_sub - 1 + n_grp - 1)

    def halo_copy(target_sub):
        return pltpu.make_async_remote_copy(
            src_ref=part_ref.at[:, pl.ds(own_count, band)],
            dst_ref=halo,
            send_sem=halo_send,
            recv_sem=halo_recv,
            device_id=(my_grp, target_sub),
            device_id_type=MESH,
        )

    @pl.when(my_sub < n_sub - 1)
    def _():
        halo_copy(my_sub + 1).start()

    @pl.when(my_sub > 0)
    def _():
        halo_copy(my_sub - 1).wait_recv()
        image_ref[:, pl.ds(0, band)] = image_ref[:, pl.ds(0, band)] + halo[...]

    residual_head = res_ref[:, pl.ds(0, band)]
    image_head = image_ref[:, pl.ds(0, band)]
    along = along_rest + jnp.sum(residual_head * image_head, axis=1, keepdims=True)
    energy = energy_rest + jnp.sum(image_head * image_head, axis=1, keepdims=True)

    width = rows // 3
    along = along[0:width] + along[width : 2 * width] + along[2 * width :]
    energy = energy[0:width] + energy[width : 2 * width] + energy[2 * width :]
    lane = lax.broadcasted_iota(jnp.int32, (8, 128), 1)
    block = jnp.zeros((8, 128), jnp.float32)
    for k in range(width // 8):
        block = jnp.where(lane == k, along[8 * k : 8 * k + 8], block)
        block = jnp.where(lane == width // 8 + k, energy[8 * k : 8 * k + 8], block)

    def exchange(value, first, count, my_index, device_of):
        slots[first + my_index] = value
        sends = []
        for d in range(1, count):
            copy = pltpu.make_async_remote_copy(
                src_ref=slots.at[first + my_index],
                dst_ref=slots.at[first + my_index],
                send_sem=send_sem.at[first + d],
                recv_sem=recv_sem.at[first + my_index],
                device_id=device_of((my_index + d) % count),
                device_id_type=MESH,
            )
            copy.start()
            sends.append(copy)
        for d in range(1, count):
            source = (my_index + count - d) % count
            pltpu.make_async_remote_copy(
                src_ref=slots.at[first + source],
                dst_ref=slots.at[first + source],
                send_sem=send_sem.at[first + d],
                recv_sem=recv_sem.at[first + source],
                device_id=device_of(source),
                device_id_type=MESH,
            ).wait_recv()
        for copy in sends:
            copy.wait_send()
        total = slots[first]
        for i in range(1, count):
            total = total + slots[first + i]
        return total

    partial_sum = exchange(block, 0, n_grp, my_grp, lambda i: (i, my_sub))
    sums_ref[...] = exchange(partial_sum, n_grp, n_sub, my_sub, lambda i: (my_grp, i))

    @pl.when(my_sub < n_sub - 1)
    def _():
        halo_copy(my_sub + 1).wait_send()


def image_and_sums(residual, partial_sum, call):
    n_grp = lax.axis_size("grp")
    n_sub = lax.axis_size("sub")
    rows, own_count = residual.shape
    band = partial_sum.shape[1] - own_count
    width = rows // 3
    image, sums = pl.pallas_call(
        functools.partial(image_sums_kernel, n_grp, n_sub),
        out_shape=(
            jax.ShapeDtypeStruct((rows, own_count), jnp.float32),
            jax.ShapeDtypeStruct((8, 128), jnp.float32),
        ),
        in_specs=[pl.BlockSpec(memory_space=pltpu.VMEM)] * 2,
        out_specs=(pl.BlockSpec(memory_space=pltpu.VMEM),) * 2,
        scratch_shapes=[
            pltpu.VMEM((rows, band), jnp.float32),
            pltpu.VMEM((n_sub + n_grp, 8, 128), jnp.float32),
            pltpu.SemaphoreType.DMA((n_sub + n_grp,)),
            pltpu.SemaphoreType.DMA((n_sub + n_grp,)),
            pltpu.SemaphoreType.DMA(()),
            pltpu.SemaphoreType.DMA(()),
        ],
        compiler_params=pltpu.CompilerParams(collective_id=call, has_side_effects=True),
    )(residual, partial_sum)
    columns = width // 8
    along = sums[:, :columns].T.reshape(width)
    energy = sums[:, columns : 2 * columns].T.reshape(width)
    return image, along, energy


def column_sums(first, second):
    return jnp.sum((first * second).reshape(3, -1, first.shape[1]), axis=(0, 2))


def update(solution, residual, image, along, energy):
    alpha = along / (energy + epsilon)
    scale_rows = jnp.tile(alpha, 3)[:, None]
    return (solution + scale_rows * residual, residual - scale_rows * image)


def shards(rhs, blocks, owners, conn):
    groups = lax.axis_size("grp")
    held = blocks.shape[0]
    capacity = max(2, 3 * held // 8)
    send_blocks, send_links = place_blocks(blocks, owners, conn, groups, capacity)
    got_blocks, got_links = (
        lax.all_to_all(send_blocks, "grp", split_axis=0, concat_axis=0, tiled=True),
        lax.all_to_all(send_links, "grp", split_axis=0, concat_axis=0, tiled=True),
    )
    matrices = got_blocks[:, :, :6561].reshape(groups * capacity, 81, 81)
    residual = rhs
    solution = jnp.zeros(rhs.shape, jnp.float32)
    own_count = rhs.shape[1]
    band_width = 2 * held
    local_links = jnp.clip(
        got_links - lax.axis_index("sub") * own_count, 0, own_count + band_width - 1
    ).astype(jnp.int32)
    places = jnp.arange(own_count + band_width, dtype=jnp.int32)
    selector = (places[:, None] == local_links.reshape(1, -1)).astype(jnp.bfloat16)
    for step in range(STEPS):
        rounded = residual.astype(jnp.bfloat16)
        upper = passed_along(rounded[:, :band_width], "sub", -1)
        split = local_links.reshape(1, -1) if step else None
        partial_sum = element_products(matrices, selector, rounded, upper, split)
        image, along, energy = image_and_sums(residual, partial_sum, step)
        solution, residual = update(solution, residual, image, along, energy)
    return (solution, residual)


def solution(mesh):
    return jax.shard_map(
        shards,
        mesh=mesh,
        in_specs=(
            P(None, ("grp", "sub")),
            P(("grp", "sub"), None),
            P(("grp", "sub"), None),
            P(("grp", "sub"), None),
        ),
        out_specs=(P(None, ("grp", "sub")), P(None, ("grp", "sub"))),
        check_vma=False,
    )
```

```python
import functools

import jax
import jax.numpy as jnp
from jax import lax
from jax.experimental import pallas as pl
from jax.experimental.pallas import tpu as pltpu
from jax.sharding import PartitionSpec as P

MESH = pl.DeviceIdType.MESH

STEPS = 2


epsilon = 1e-06


def passed_along(block, axis, distance):
    devices = range(lax.axis_size(axis))
    route = [(i - distance, i) for i in devices if i - distance in devices]
    return lax.ppermute(block, axis, route)


def place_blocks(blocks, owners, conn, groups, capacity):
    owner_group = owners[:, 0]
    onehot = (owner_group[:, None] == jnp.arange(groups, dtype=jnp.int32)[None, :]).astype(
        jnp.int32
    )
    rows = jnp.arange(owner_group.shape[0], dtype=jnp.int32)
    earlier = (rows[:, None] > rows[None, :]).astype(jnp.bfloat16)
    before = jnp.dot(earlier, onehot.astype(jnp.bfloat16), preferred_element_type=jnp.float32)
    position = jnp.sum(before.astype(jnp.int32) * onehot, axis=1)
    target = owner_group * capacity + position
    send_blocks = (
        jnp.zeros((groups * capacity, blocks.shape[1]), blocks.dtype).at[target].set(blocks)
    )
    send_links = jnp.zeros((groups * capacity, conn.shape[1]), jnp.int32).at[target].set(conn)
    return (send_blocks.reshape(groups, capacity, -1), send_links.reshape(groups, -1))


def element_products(matrices, selector, own_field, upper_field, split):
    rows = own_field.shape[0]
    own_count = own_field.shape[1]
    count = matrices.shape[0]
    contract = (((0,), (1,)), ((), ()))
    if split is not None:
        links = split
        own_places = jnp.arange(own_count, dtype=jnp.int32)
        upper_places = jnp.arange(upper_field.shape[1], dtype=jnp.int32) + own_count
        own_selector = (own_places[:, None] == links).astype(jnp.bfloat16)
        upper_selector = (upper_places[:, None] == links).astype(jnp.bfloat16)
        picked = lax.dot_general(
            own_selector, own_field, contract, preferred_element_type=jnp.float32
        )
        picked = picked + lax.dot_general(
            upper_selector, upper_field, contract, preferred_element_type=jnp.float32
        )
    else:
        field = jnp.concatenate([own_field, upper_field], axis=1)
        picked = lax.dot_general(selector, field, contract, preferred_element_type=jnp.float32)
    picked = picked.astype(jnp.bfloat16)
    picked = picked.reshape(count, 81, rows // 3)
    result = jnp.einsum("sab,sao->sbo", matrices, picked, preferred_element_type=jnp.float32)
    result = result.reshape(count * 27, rows)
    high_part = result.astype(jnp.bfloat16)
    low_part = (result - high_part.astype(jnp.float32)).astype(jnp.bfloat16)
    parts = jnp.concatenate([high_part, low_part], axis=1)
    acc = jnp.dot(selector, parts, preferred_element_type=jnp.float32)
    return (acc[:, :rows] + acc[:, rows:]).T


def image_sums_kernel(
    n_grp, n_sub, res_ref, part_ref, image_ref, sums_ref,
    halo, slots, send_sem, recv_sem, halo_send, halo_recv,
):
    my_grp = lax.axis_index("grp")
    my_sub = lax.axis_index("sub")
    own_count = image_ref.shape[1]
    band = halo.shape[1]
    rows = res_ref.shape[0]
    barrier = pltpu.get_barrier_semaphore()
    for d in range(1, n_sub):
        target = (my_grp, (my_sub + d) % n_sub)
        pl.semaphore_signal(barrier, inc=1, device_id=target, device_id_type=MESH)
    for d in range(1, n_grp):
        target = ((my_grp + d) % n_grp, my_sub)
        pl.semaphore_signal(barrier, inc=1, device_id=target, device_id_type=MESH)
    image_ref[...] = part_ref[:, pl.ds(0, own_count)]
    rest = own_count - band
    residual_rest = res_ref[:, pl.ds(band, rest)]
    image_rest = part_ref[:, pl.ds(band, rest)]
    along_rest = jnp.sum(residual_rest * image_rest, axis=1, keepdims=True)
    energy_rest = jnp.sum(image_rest * image_rest, axis=1, keepdims=True)
    pl.semaphore_wait(barrier, n_sub - 1 + n_grp - 1)

    def halo_copy(target_sub):
        return pltpu.make_async_remote_copy(
            src_ref=part_ref.at[:, pl.ds(own_count, band)],
            dst_ref=halo,
            send_sem=halo_send,
            recv_sem=halo_recv,
            device_id=(my_grp, target_sub),
            device_id_type=MESH,
        )

    @pl.when(my_sub < n_sub - 1)
    def _():
        halo_copy(my_sub + 1).start()

    @pl.when(my_sub > 0)
    def _():
        halo_copy(my_sub - 1).wait_recv()
        image_ref[:, pl.ds(0, band)] = image_ref[:, pl.ds(0, band)] + halo[...]

    residual_head = res_ref[:, pl.ds(0, band)]
    image_head = image_ref[:, pl.ds(0, band)]
    along = along_rest + jnp.sum(residual_head * image_head, axis=1, keepdims=True)
    energy = energy_rest + jnp.sum(image_head * image_head, axis=1, keepdims=True)

    width = rows // 3
    along = along[0:width] + along[width : 2 * width] + along[2 * width :]
    energy = energy[0:width] + energy[width : 2 * width] + energy[2 * width :]
    lane = lax.broadcasted_iota(jnp.int32, (8, 128), 1)
    block = jnp.zeros((8, 128), jnp.float32)
    for k in range(width // 8):
        block = jnp.where(lane == k, along[8 * k : 8 * k + 8], block)
        block = jnp.where(lane == width // 8 + k, energy[8 * k : 8 * k + 8], block)

    def exchange(value, first, count, my_index, device_of):
        slots[first + my_index] = value
        sends = []
        for d in range(1, count):
            copy = pltpu.make_async_remote_copy(
                src_ref=slots.at[first + my_index],
                dst_ref=slots.at[first + my_index],
                send_sem=send_sem.at[first + d],
                recv_sem=recv_sem.at[first + my_index],
                device_id=device_of((my_index + d) % count),
                device_id_type=MESH,
            )
            copy.start()
            sends.append(copy)
        for d in range(1, count):
            source = (my_index + count - d) % count
            pltpu.make_async_remote_copy(
                src_ref=slots.at[first + source],
                dst_ref=slots.at[first + source],
                send_sem=send_sem.at[first + d],
                recv_sem=recv_sem.at[first + source],
                device_id=device_of(source),
                device_id_type=MESH,
            ).wait_recv()
        for copy in sends:
            copy.wait_send()
        total = slots[first]
        for i in range(1, count):
            total = total + slots[first + i]
        return total

    partial_sum = exchange(block, 0, n_grp, my_grp, lambda i: (i, my_sub))
    sums_ref[...] = exchange(partial_sum, n_grp, n_sub, my_sub, lambda i: (my_grp, i))

    @pl.when(my_sub < n_sub - 1)
    def _():
        halo_copy(my_sub + 1).wait_send()


def image_and_sums(residual, partial_sum, call):
    n_grp = lax.axis_size("grp")
    n_sub = lax.axis_size("sub")
    rows, own_count = residual.shape
    band = partial_sum.shape[1] - own_count
    width = rows // 3
    image, sums = pl.pallas_call(
        functools.partial(image_sums_kernel, n_grp, n_sub),
        out_shape=(
            jax.ShapeDtypeStruct((rows, own_count), jnp.float32),
            jax.ShapeDtypeStruct((8, 128), jnp.float32),
        ),
        in_specs=[pl.BlockSpec(memory_space=pltpu.VMEM)] * 2,
        out_specs=(pl.BlockSpec(memory_space=pltpu.VMEM),) * 2,
        scratch_shapes=[
            pltpu.VMEM((rows, band), jnp.float32),
            pltpu.VMEM((n_sub + n_grp, 8, 128), jnp.float32),
            pltpu.SemaphoreType.DMA((n_sub + n_grp,)),
            pltpu.SemaphoreType.DMA((n_sub + n_grp,)),
            pltpu.SemaphoreType.DMA(()),
            pltpu.SemaphoreType.DMA(()),
        ],
        compiler_params=pltpu.CompilerParams(collective_id=call, has_side_effects=True),
    )(residual, partial_sum)
    columns = width // 8
    along = sums[:, :columns].T.reshape(width)
    energy = sums[:, columns : 2 * columns].T.reshape(width)
    return image, along, energy


def column_sums(first, second):
    return jnp.sum((first * second).reshape(3, -1, first.shape[1]), axis=(0, 2))


def update(solution, residual, image, along, energy):
    alpha = along / (energy + epsilon)
    scale_rows = jnp.tile(alpha, 3)[:, None]
    return (solution + scale_rows * residual, residual - scale_rows * image)


def shards(rhs, blocks, owners, conn):
    groups = lax.axis_size("grp")
    held = blocks.shape[0]
    capacity = max(2, 3 * held // 8)
    send_blocks, send_links = place_blocks(blocks, owners, conn, groups, capacity)
    got_blocks, got_links = (
        lax.all_to_all(send_blocks, "grp", split_axis=0, concat_axis=0, tiled=True),
        lax.all_to_all(send_links, "grp", split_axis=0, concat_axis=0, tiled=True),
    )
    matrices = got_blocks[:, :, :6561].reshape(groups * capacity, 81, 81)
    residual = rhs
    solution = jnp.zeros(rhs.shape, jnp.float32)
    own_count = rhs.shape[1]
    band_width = 2 * held
    local_links = jnp.clip(
        got_links - lax.axis_index("sub") * own_count, 0, own_count + band_width - 1
    ).astype(jnp.int32)
    places = jnp.arange(own_count + band_width, dtype=jnp.int32)
    selector = (places[:, None] == local_links.reshape(1, -1)).astype(jnp.bfloat16)
    for step in range(STEPS):
        rounded = residual.astype(jnp.bfloat16)
        upper = passed_along(rounded[:, :band_width], "sub", -1)
        split = local_links.reshape(1, -1) if step else None
        partial_sum = element_products(matrices, selector, rounded, upper, split)
        image, along, energy = image_and_sums(residual, partial_sum, step)
        solution, residual = update(solution, residual, image, along, energy)
    return (solution, residual)


def solution(mesh):
    return jax.shard_map(
        shards,
        mesh=mesh,
        in_specs=(
            P(None, ("grp", "sub")),
            P(("grp", "sub"), None),
            P(("grp", "sub"), None),
            P(("grp", "sub"), None),
        ),
        out_specs=(P(None, ("grp", "sub")), P(None, ("grp", "sub"))),
        check_vma=False,
    )
```

```python
import functools

import jax
import jax.numpy as jnp
from jax import lax
from jax.experimental import pallas as pl
from jax.experimental.pallas import tpu as pltpu
from jax.sharding import PartitionSpec as P

MESH = pl.DeviceIdType.MESH

STEPS = 2


epsilon = 1e-06


def passed_along(block, axis, distance):
    devices = range(lax.axis_size(axis))
    route = [(i - distance, i) for i in devices if i - distance in devices]
    return lax.ppermute(block, axis, route)


def place_blocks(blocks, owners, conn, groups, capacity):
    owner_group = owners[:, 0]
    onehot = (owner_group[:, None] == jnp.arange(groups, dtype=jnp.int32)[None, :]).astype(
        jnp.int32
    )
    rows = jnp.arange(owner_group.shape[0], dtype=jnp.int32)
    earlier = (rows[:, None] > rows[None, :]).astype(jnp.bfloat16)
    before = jnp.dot(earlier, onehot.astype(jnp.bfloat16), preferred_element_type=jnp.float32)
    position = jnp.sum(before.astype(jnp.int32) * onehot, axis=1)
    target = owner_group * capacity + position
    send_blocks = (
        jnp.zeros((groups * capacity, blocks.shape[1]), blocks.dtype).at[target].set(blocks)
    )
    send_links = jnp.zeros((groups * capacity, conn.shape[1]), jnp.int32).at[target].set(conn)
    return (send_blocks.reshape(groups, capacity, -1), send_links.reshape(groups, -1))


def element_products(matrices, selector, own_field, upper_field, split):
    rows = own_field.shape[0]
    own_count = own_field.shape[1]
    count = matrices.shape[0]
    contract = (((0,), (1,)), ((), ()))
    if split is not None:
        links = split
        own_places = jnp.arange(own_count, dtype=jnp.int32)
        upper_places = jnp.arange(upper_field.shape[1], dtype=jnp.int32) + own_count
        own_selector = (own_places[:, None] == links).astype(jnp.bfloat16)
        upper_selector = (upper_places[:, None] == links).astype(jnp.bfloat16)
        picked = lax.dot_general(
            own_selector, own_field, contract, preferred_element_type=jnp.float32
        )
        picked = picked + lax.dot_general(
            upper_selector, upper_field, contract, preferred_element_type=jnp.float32
        )
    else:
        field = jnp.concatenate([own_field, upper_field], axis=1)
        picked = lax.dot_general(selector, field, contract, preferred_element_type=jnp.float32)
    picked = picked.astype(jnp.bfloat16)
    picked = picked.reshape(count, 81, rows // 3)
    result = jnp.einsum("sab,sao->sbo", matrices, picked, preferred_element_type=jnp.float32)
    result = result.reshape(count * 27, rows)
    high_part = result.astype(jnp.bfloat16)
    low_part = (result - high_part.astype(jnp.float32)).astype(jnp.bfloat16)
    parts = jnp.concatenate([high_part, low_part], axis=1)
    acc = jnp.dot(selector, parts, preferred_element_type=jnp.float32)
    return (acc[:, :rows] + acc[:, rows:]).T


def image_sums_kernel(
    n_grp, n_sub, res_ref, part_ref, image_ref, sums_ref,
    halo, slots, send_sem, recv_sem, halo_send, halo_recv,
):
    my_grp = lax.axis_index("grp")
    my_sub = lax.axis_index("sub")
    own_count = image_ref.shape[1]
    band = halo.shape[1]
    rows = res_ref.shape[0]
    barrier = pltpu.get_barrier_semaphore()
    for d in range(1, n_sub):
        target = (my_grp, (my_sub + d) % n_sub)
        pl.semaphore_signal(barrier, inc=1, device_id=target, device_id_type=MESH)
    for d in range(1, n_grp):
        target = ((my_grp + d) % n_grp, my_sub)
        pl.semaphore_signal(barrier, inc=1, device_id=target, device_id_type=MESH)
    pl.semaphore_wait(barrier, n_sub - 1 + n_grp - 1)

    def halo_copy(target_sub):
        return pltpu.make_async_remote_copy(
            src_ref=part_ref.at[:, pl.ds(own_count, band)],
            dst_ref=halo,
            send_sem=halo_send,
            recv_sem=halo_recv,
            device_id=(my_grp, target_sub),
            device_id_type=MESH,
        )

    @pl.when(my_sub < n_sub - 1)
    def _():
        halo_copy(my_sub + 1).start()

    image_ref[...] = part_ref[:, pl.ds(0, own_count)]
    rest = own_count - band
    residual_rest = res_ref[:, pl.ds(band, rest)]
    image_rest = part_ref[:, pl.ds(band, rest)]
    along_rest = jnp.sum(residual_rest * image_rest, axis=1, keepdims=True)
    energy_rest = jnp.sum(image_rest * image_rest, axis=1, keepdims=True)
    @pl.when(my_sub > 0)
    def _():
        halo_copy(my_sub - 1).wait_recv()
        image_ref[:, pl.ds(0, band)] = image_ref[:, pl.ds(0, band)] + halo[...]

    residual_head = res_ref[:, pl.ds(0, band)]
    image_head = image_ref[:, pl.ds(0, band)]
    along = along_rest + jnp.sum(residual_head * image_head, axis=1, keepdims=True)
    energy = energy_rest + jnp.sum(image_head * image_head, axis=1, keepdims=True)

    width = rows // 3
    along = along[0:width] + along[width : 2 * width] + along[2 * width :]
    energy = energy[0:width] + energy[width : 2 * width] + energy[2 * width :]
    lane = lax.broadcasted_iota(jnp.int32, (8, 128), 1)
    block = jnp.zeros((8, 128), jnp.float32)
    for k in range(width // 8):
        block = jnp.where(lane == k, along[8 * k : 8 * k + 8], block)
        block = jnp.where(lane == width // 8 + k, energy[8 * k : 8 * k + 8], block)

    def exchange(value, first, count, my_index, device_of):
        slots[first + my_index] = value
        sends = []
        for d in range(1, count):
            copy = pltpu.make_async_remote_copy(
                src_ref=slots.at[first + my_index],
                dst_ref=slots.at[first + my_index],
                send_sem=send_sem.at[first + d],
                recv_sem=recv_sem.at[first + my_index],
                device_id=device_of((my_index + d) % count),
                device_id_type=MESH,
            )
            copy.start()
            sends.append(copy)
        for d in range(1, count):
            source = (my_index + count - d) % count
            pltpu.make_async_remote_copy(
                src_ref=slots.at[first + source],
                dst_ref=slots.at[first + source],
                send_sem=send_sem.at[first + d],
                recv_sem=recv_sem.at[first + source],
                device_id=device_of(source),
                device_id_type=MESH,
            ).wait_recv()
        for copy in sends:
            copy.wait_send()
        total = slots[first]
        for i in range(1, count):
            total = total + slots[first + i]
        return total

    partial_sum = exchange(block, 0, n_grp, my_grp, lambda i: (i, my_sub))
    sums_ref[...] = exchange(partial_sum, n_grp, n_sub, my_sub, lambda i: (my_grp, i))

    @pl.when(my_sub < n_sub - 1)
    def _():
        halo_copy(my_sub + 1).wait_send()


def image_and_sums(residual, partial_sum, call):
    n_grp = lax.axis_size("grp")
    n_sub = lax.axis_size("sub")
    rows, own_count = residual.shape
    band = partial_sum.shape[1] - own_count
    width = rows // 3
    image, sums = pl.pallas_call(
        functools.partial(image_sums_kernel, n_grp, n_sub),
        out_shape=(
            jax.ShapeDtypeStruct((rows, own_count), jnp.float32),
            jax.ShapeDtypeStruct((8, 128), jnp.float32),
        ),
        in_specs=[pl.BlockSpec(memory_space=pltpu.VMEM)] * 2,
        out_specs=(pl.BlockSpec(memory_space=pltpu.VMEM),) * 2,
        scratch_shapes=[
            pltpu.VMEM((rows, band), jnp.float32),
            pltpu.VMEM((n_sub + n_grp, 8, 128), jnp.float32),
            pltpu.SemaphoreType.DMA((n_sub + n_grp,)),
            pltpu.SemaphoreType.DMA((n_sub + n_grp,)),
            pltpu.SemaphoreType.DMA(()),
            pltpu.SemaphoreType.DMA(()),
        ],
        compiler_params=pltpu.CompilerParams(collective_id=call, has_side_effects=True),
    )(residual, partial_sum)
    columns = width // 8
    along = sums[:, :columns].T.reshape(width)
    energy = sums[:, columns : 2 * columns].T.reshape(width)
    return image, along, energy


def column_sums(first, second):
    return jnp.sum((first * second).reshape(3, -1, first.shape[1]), axis=(0, 2))


def update(solution, residual, image, along, energy):
    alpha = along / (energy + epsilon)
    scale_rows = jnp.tile(alpha, 3)[:, None]
    return (solution + scale_rows * residual, residual - scale_rows * image)


def shards(rhs, blocks, owners, conn):
    groups = lax.axis_size("grp")
    held = blocks.shape[0]
    capacity = max(2, 3 * held // 8)
    send_blocks, send_links = place_blocks(blocks, owners, conn, groups, capacity)
    got_blocks, got_links = (
        lax.all_to_all(send_blocks, "grp", split_axis=0, concat_axis=0, tiled=True),
        lax.all_to_all(send_links, "grp", split_axis=0, concat_axis=0, tiled=True),
    )
    matrices = got_blocks[:, :, :6561].reshape(groups * capacity, 81, 81)
    residual = rhs
    solution = jnp.zeros(rhs.shape, jnp.float32)
    own_count = rhs.shape[1]
    band_width = 2 * held
    local_links = jnp.clip(
        got_links - lax.axis_index("sub") * own_count, 0, own_count + band_width - 1
    ).astype(jnp.int32)
    places = jnp.arange(own_count + band_width, dtype=jnp.int32)
    selector = (places[:, None] == local_links.reshape(1, -1)).astype(jnp.bfloat16)
    for step in range(STEPS):
        rounded = residual.astype(jnp.bfloat16)
        upper = passed_along(rounded[:, :band_width], "sub", -1)
        split = local_links.reshape(1, -1) if step else None
        partial_sum = element_products(matrices, selector, rounded, upper, split)
        image, along, energy = image_and_sums(residual, partial_sum, step)
        solution, residual = update(solution, residual, image, along, energy)
    return (solution, residual)


def solution(mesh):
    return jax.shard_map(
        shards,
        mesh=mesh,
        in_specs=(
            P(None, ("grp", "sub")),
            P(("grp", "sub"), None),
            P(("grp", "sub"), None),
            P(("grp", "sub"), None),
        ),
        out_specs=(P(None, ("grp", "sub")), P(None, ("grp", "sub"))),
        check_vma=False,
    )
```
